128 devices in a mesh: gx: 32 (over y, x, core), ba: 4 (over z).
Axes of the slice: x: 4, y: 4, z: 4, core: 2. Of those that a mesh axis runs over, the one named last changes fastest.
Arguments:
- phi_start: float32 [64, 16, 256, 256], P('gx', 'ba'), may hold values from -6 to 6
- coeff: float32 [64, 256, 256], P('gx'), may hold values from 1 to 3
- forward: float32 [2, 2, 64, 256, 256], P(None, None, None, 'gx'), may hold values from -6 to 6
- rates: float32 [16], P('ba'), may hold values from 0.02 to 0.2
- speeds: float32 [16], P('ba'), may hold values from 0.5 to 2
- shares: float32 [16], P('ba'), may hold values from 0.02 to 0.12
Outputs:
- phi_out: float32 [64, 16, 256, 256], P('gx', 'ba')
- grad: float32 [64, 12, 16], P('gx', None, 'ba')
The draws below stay inside these ranges and needn't reach their ends.
All inputs are finite; a program needn't handle non-finite values.
Results may differ from the reference program's by a relative error of at most 0.00026.
Values sent between devices are 32-bit elements; how exact they have to be, the bound alone decides.
A program may use at most 128 MiB of HBM per device.

```python
import math
import jax
import jax.numpy as jnp
from jax import lax

NX = 256
NY = 256
Z = 64
STEPS = 2
BANDS = 16


def block_levels(rng, extent, pieces, least, largest):
    gain = 1.0
    for axis_at, shards_of in pieces:
        heights = jax.random.uniform(jax.random.fold_in(jax.random.fold_in(rng, 6), axis_at), (shards_of,), jnp.float32, least / len(pieces), largest / len(pieces))
        gain = gain * jnp.repeat(jnp.exp(heights), extent[axis_at] // shards_of).reshape((-1,) + (1,) * (len(extent) - 1 - axis_at))
    return gain


def scatter_about(own_key, dims, scale, limit, split=(), held_as=jnp.bfloat16):
    gain = block_levels(own_key, dims, split, -0.22, 0.18) if split else 1.0
    result = jax.random.normal(own_key, dims, jnp.float32) * scale * gain
    return jnp.minimum(jnp.maximum(result, -limit), limit).astype(held_as)


def setup_inputs(seed: int = 0) -> dict:
    splits = jax.random.split(jax.random.key(seed), 7)
    phi_start = scatter_about(splits[0], (Z, BANDS, NX, NY), 1.0, 6.0, ((0, 32), (1, 4)), jnp.float32)
    coeff = jnp.clip(1.0 + 2.0 * jax.random.uniform(splits[1], (Z, NX, NY), jnp.float32) ** block_levels(splits[1], (Z, NX, NY), ((0, 32),), -0.2, 0.2), 1.0, 3.0)
    forward = scatter_about(splits[2], (STEPS, 2, Z, NX, NY), 1.0, 6.0, ((3, 32),), jnp.float32)
    rates = jnp.clip(jnp.exp(math.log(0.2) - 2.3025851 * jax.random.uniform(splits[3], (BANDS,), jnp.float32) ** block_levels(splits[3], (BANDS,), ((0, 4),), -0.2, 0.2)), 0.02, 0.2)
    speeds = jnp.clip(jnp.exp(math.log(2.0) - 1.3862944 * jax.random.uniform(splits[4], (BANDS,), jnp.float32) ** block_levels(splits[4], (BANDS,), ((0, 4),), -0.2, 0.2)), 0.5, 2.0)
    shares = jnp.clip(jnp.exp(math.log(0.12) - 1.7917595 * jax.random.uniform(splits[5], (BANDS,), jnp.float32) ** block_levels(splits[5], (BANDS,), ((0, 4),), -0.2, 0.2)), 0.02, 0.12)
    return dict(phi_start=phi_start, coeff=coeff, forward=forward, rates=rates, speeds=speeds, shares=shares)


def quadrature():
    level = jnp.arange(6).astype(jnp.float32)
    polar = 0.2 + 0.15 * level
    cosine = jnp.concatenate([-polar, polar])
    azimuth = jnp.concatenate([level * (math.pi / 3.0) + math.pi / 6.0, level * (math.pi / 3.0)])
    sine = jnp.sqrt(1.0 - cosine * cosine)
    return (cosine, sine * jnp.cos(azimuth), sine * jnp.sin(azimuth))

def frequency(count, start, length):
    index = jnp.arange(length, dtype=jnp.int32) + start
    signed = (index + count // 2) % count - count // 2
    return signed.astype(jnp.float32) * (1.5 * 2.0 * math.pi / count)

def sweep(source_re, source_im, inv_re, inv_im, couple, start_re, start_im, target_re, target_im, scale, reverse):
    depth = source_re.shape[0]
    blocks = depth // 8

    def fold(value):
        return value.reshape((blocks, 8) + value.shape[1:])
    cells = list(range(7, -1, -1)) if reverse else list(range(8))

    def block(carried, inputs):
        psi_real, psi_imag = carried
        rows_re, rows_im, aims_re, aims_im = inputs
        phi_real = [None] * 8
        phi_imag = [None] * 8
        sums = [None] * 8
        for cell in cells:
            sum_real = rows_re[cell] + couple * psi_real
            sum_imag = rows_im[cell] + couple * psi_imag
            psi_real = inv_re * sum_real - inv_im * sum_imag
            psi_imag = inv_re * sum_imag + inv_im * sum_real
            phi_real[cell] = lax.optimization_barrier(jnp.sum(psi_real, axis=0)) / 12.0
            phi_imag[cell] = lax.optimization_barrier(jnp.sum(psi_imag, axis=0)) / 12.0
            sums[cell] = lax.optimization_barrier(jnp.sum(psi_real * aims_re[cell] + psi_imag * aims_im[cell], axis=(2, 3))) * scale
        return ((psi_real, psi_imag), (jnp.stack(phi_real), jnp.stack(phi_imag), jnp.stack(sums)))
    carried, outputs = lax.scan(block, (start_re, start_im), (fold(source_re), fold(source_im), fold(target_re), fold(target_im)), reverse=reverse)

    def unfold(value):
        return value.reshape((depth,) + value.shape[2:])
    return (carried, unfold(outputs[0]), unfold(outputs[1]), unfold(outputs[2]))

def solve_modes(spec_re, spec_im, rates, speeds, shares, freq_x, freq_y, target_re, target_im, scale, wall_sum):
    cosine, along_x, along_y = quadrature()
    rate = rates[:, None, None]
    speed = speeds[:, None, None]
    source_re = spec_re * rate
    source_im = spec_im * rate
    wave = speed[None] * (along_x[:, None, None, None] * freq_x[:, None] + along_y[:, None, None, None] * freq_y[None, :])
    couple = jnp.abs(cosine)[:, None, None, None] * speed[None]
    real_part = rate[None] + couple
    denom = real_part * real_part + wave * wave
    inv_re = real_part / denom
    inv_im = -wave / denom
    zeros = jnp.zeros_like(inv_re[:6])
    down_end, down_re, down_im, down_grad = sweep(source_re, source_im, inv_re[:6], inv_im[:6], couple[:6], zeros, zeros, target_re, target_im, scale, True)
    weight = (jnp.abs(cosine[:6]) / 12.0)[:, None, None, None]
    flux_re = lax.optimization_barrier(jnp.sum(weight * down_end[0], axis=(0, 1)))
    flux_im = lax.optimization_barrier(jnp.sum(weight * down_end[1], axis=(0, 1)))
    flux_re, flux_im = wall_sum(flux_re, flux_im)
    share = shares[:, None, None]
    start_re = jnp.broadcast_to(share * flux_re, zeros.shape)
    start_im = jnp.broadcast_to(share * flux_im, zeros.shape)
    up_end, up_re, up_im, up_grad = sweep(source_re, source_im, inv_re[6:], inv_im[6:], couple[6:], start_re, start_im, target_re, target_im, scale, False)
    return (down_re + up_re, down_im + up_im, jnp.concatenate([down_grad, up_grad], axis=1))

def keep_flux(flux_re, flux_im):
    return (flux_re, flux_im)

def reference(phi_start, coeff, forward, rates, speeds, shares):
    phi = phi_start
    freq_x = frequency(NX, 0, NX)
    freq_y = frequency(NY, 0, NY)
    scale = 1.0 / NX
    grad = jnp.zeros((Z, 12, BANDS), jnp.float32)
    for step in range(STEPS):
        spec = jnp.fft.fft2(phi, axes=(2, 3), norm='ortho')
        new_re, new_im, grad_step = solve_modes(jnp.real(spec), jnp.imag(spec), rates, speeds, shares, freq_x, freq_y, forward[step, 0], forward[step, 1], scale, keep_flux)
        grad = grad + grad_step
        back = jnp.real(jnp.fft.ifft2(lax.complex(new_re, new_im), axes=(2, 3), norm='ortho'))
        phi = coeff[:, None] * back
    return (phi, grad)
```

```python
import functools
import math

import jax
import jax.numpy as jnp
import numpy as np
from jax import lax
from jax.experimental import pallas as pl
from jax.experimental.pallas import tpu as pltpu
from jax.sharding import PartitionSpec as P

MESH = pl.DeviceIdType.MESH
N = 256
HALF = 128
GX = 32
BA = 4
ROWS = 8
BASE = 1.5 * 2.0 * math.pi / N


def quadrature():
    level = np.arange(6)
    polar = 0.2 + 0.15 * level
    cosine = np.concatenate([-polar, polar])
    azimuth = np.concatenate([level * (math.pi / 3.0) + math.pi / 6.0, level * (math.pi / 3.0)])
    sine = np.sqrt(1.0 - cosine * cosine)
    return cosine, sine * np.cos(azimuth), sine * np.sin(azimuth)


COS, SX, SY = quadrature()


def halves(table):
    table = jnp.asarray(table, jnp.float32)
    high = table.astype(jnp.bfloat16)
    return high, (table - high.astype(jnp.float32)).astype(jnp.bfloat16)


def np_halves(table):
    table = np.asarray(table, np.float32)
    high = table.astype(jnp.bfloat16)
    low = (table - high.astype(np.float32)).astype(jnp.bfloat16)
    return [jnp.asarray(high), jnp.asarray(low)]


def tables():
    index = np.arange(N)
    angle = (index[:, None] * index[None, :] % N) * (2.0 * np.pi / N)
    cos, sin = np.cos(angle) / 16.0, np.sin(angle) / 16.0
    rows = np.concatenate([cos[:, :HALF], -sin[:, :HALF]], axis=1)
    rows[:, HALF] = cos[:, HALF]
    back = np.concatenate([2.0 * cos[:HALF], -2.0 * sin[:HALF]], axis=0)
    back[0] = cos[0]
    back[HALF] = cos[HALF]
    return np_halves(rows), np_halves(back), np_halves(cos), np_halves(sin)


def split(value):
    high = value.astype(jnp.bfloat16)
    return high, (value - high.astype(jnp.float32)).astype(jnp.bfloat16)


def product(left, right):
    lh, ll = left
    rh, rl = right
    dot = functools.partial(jnp.dot, preferred_element_type=jnp.float32)
    return dot(lh, rh) + (dot(ll, rh) + dot(lh, rl))


def forward_kernel(phi, wh, wl, ch, cl, sh, sl, out, edge):
    edge[...] = jnp.zeros_like(edge)
    cos, sin = (ch[...], cl[...]), (sh[...], sl[...])
    inner = lax.broadcasted_iota(jnp.int32, (N, HALF), 1) != 0
    row = lax.broadcasted_iota(jnp.int32, (ROWS, N), 0)
    sign = jnp.where(lax.broadcasted_iota(jnp.int32, (ROWS, N), 1) % 2 == 0, 1.0 / 16.0, -1.0 / 16.0)

    def plane(p, carry):
        zz, b = p // 4, p % 4
        field = split(phi[zz, b])
        rows = split(product(field, (wh[...], wl[...])))
        u = product(cos, rows)
        v = product(sin, rows)
        re = u[:, :HALF] + jnp.where(inner, v[:, HALF:], 0.0)
        im = jnp.where(inner, u[:, HALF:], 0.0) - v[:, :HALF]
        for m in range(GX):
            out[m, pl.ds(zz * 32 + b, ROWS, stride=4), :] = re[ROWS * m : ROWS * (m + 1)]
            out[m, pl.ds(64 + zz * 32 + b, ROWS, stride=4), :] = im[ROWS * m : ROWS * (m + 1)]
        pick = jnp.where(row == p, sign, 0.0).astype(jnp.bfloat16)
        nt = (((1,), (1,)), ((), ()))
        edge[...] += lax.dot_general(
            pick, field[0], nt, preferred_element_type=jnp.float32
        ) + lax.dot_general(pick, field[1], nt, preferred_element_type=jnp.float32)
        return carry

    lax.fori_loop(0, 8, plane, 0)
    line = split(edge[...])
    line_re = product(line, cos)
    line_im = -product(line, sin)
    lane = lax.broadcasted_iota(jnp.int32, (ROWS, HALF), 1)
    for m in range(GX):
        at, off = HALF * (m // 16), 8 * (m % 16)
        re, im = line_re[:, at : at + HALF], line_im[:, at : at + HALF]
        tile = jnp.where(lane < 8, pltpu.roll(re, (HALF - off) % HALF, 1), 0.0)
        tile = jnp.where((lane >= 8) & (lane < 16), pltpu.roll(re, (HALF + 8 - off) % HALF, 1), tile)
        tile = jnp.where((lane >= 64) & (lane < 72), pltpu.roll(im, (HALF + 64 - off) % HALF, 1), tile)
        tile = jnp.where((lane >= 72) & (lane < 80), pltpu.roll(im, (HALF + 72 - off) % HALF, 1), tile)
        out[m, 128:136, :] = tile


def inverse_kernel(back, coeff, wh, wl, ch, cl, sh, sl, out):
    cos, sin = (ch[...], cl[...]), (sh[...], sl[...])

    def plane(p, carry):
        zz, b = p // 4, p % 4
        re = [back[m, pl.ds(zz * 32 + b, ROWS, stride=4), :] for m in range(GX)]
        im = [back[m, pl.ds(64 + zz * 32 + b, ROWS, stride=4), :] for m in range(GX)]
        modes = split(jnp.concatenate([jnp.concatenate(re, axis=0), jnp.concatenate(im, axis=0)], axis=1))
        u = product(cos, modes)
        v = product(sin, modes)
        rows = jnp.concatenate([u[:, :HALF] - v[:, HALF:], u[:, HALF:] + v[:, :HALF]], axis=1)
        out[zz, b] = product(split(rows), (wh[...], wl[...])) * coeff[zz]
        return carry

    lax.fori_loop(0, 8, plane, 0)


def exchange_kernel(src, dst, own, send, recv):
    me, ba = lax.axis_index("gx"), lax.axis_index("ba")
    barrier = pltpu.get_barrier_semaphore()

    def greet(k, carry):
        pl.semaphore_signal(barrier, inc=1, device_id=(lax.rem(me + k, GX), ba), device_id_type=MESH)
        return carry

    lax.fori_loop(1, GX, greet, 0)
    pl.semaphore_wait(barrier, GX - 1)
    mine = pltpu.make_async_copy(src.at[me], dst.at[me], own)
    mine.start()

    def copy(k):
        to = lax.rem(me + k, GX)
        return pltpu.make_async_remote_copy(
            src_ref=src.at[to],
            dst_ref=dst.at[me],
            send_sem=send.at[k],
            recv_sem=recv.at[k],
            device_id=(to, ba),
            device_id_type=MESH,
        )

    def start(k, carry):
        copy(k).start()
        return carry

    def finish(k, carry):
        copy(k).wait()
        return carry

    lax.fori_loop(1, GX, start, 0)
    lax.fori_loop(1, GX, finish, 0)
    mine.wait()


def exchange(value, ident):
    return pl.pallas_call(
        exchange_kernel,
        out_shape=jax.ShapeDtypeStruct(value.shape, value.dtype),
        in_specs=[pl.BlockSpec(memory_space=pl.ANY)],
        out_specs=pl.BlockSpec(memory_space=pl.ANY),
        scratch_shapes=[
            pltpu.SemaphoreType.DMA,
            pltpu.SemaphoreType.DMA((GX,)),
            pltpu.SemaphoreType.DMA((GX,)),
        ],
        compiler_params=pltpu.CompilerParams(collective_id=ident, has_side_effects=True),
        name="exchange" + str(ident),
    )(value)


def solve_kernel(spec, goal, edge_goal, alpha, bands, back, grads, acc, espec, enew, flux, others, send, recv):
    gx, ba = lax.axis_index("gx"), lax.axis_index("ba")
    barrier = pltpu.get_barrier_semaphore()
    for k in range(1, BA):
        pl.semaphore_signal(barrier, inc=1, device_id=(gx, lax.rem(ba + k, BA)), device_id_type=MESH)
    sub = lax.broadcasted_iota(jnp.int32, (ROWS, HALF), 0)
    lane = lax.broadcasted_iota(jnp.int32, (ROWS, HALF), 1)
    upper = sub < 4
    rate, speed, share = bands[0], bands[1], bands[2]
    couple = [speed * float(abs(COS[d])) for d in range(6)]

    def clear(z, carry):
        for d in range(12):
            acc[z, d] = jnp.zeros((ROWS, HALF), jnp.float32)
        return carry

    lax.fori_loop(0, 64, clear, 0)

    def gather(src, carry):
        line = spec[src, 16]
        for zz in range(2):
            col = line if zz == 0 else pltpu.roll(line, 4, 0)
            col_re = jnp.where(lane < 16, col, 0.0)
            col_im = jnp.where(lane < 16, pltpu.roll(col, 64, 1), 0.0)
            espec[src, zz] = jnp.where(upper, col_re, pltpu.roll(spec[src, zz * 4], 4, 0))
            espec[src, 2 + zz] = jnp.where(upper, col_im, pltpu.roll(spec[src, 8 + zz * 4], 4, 0))
        return carry

    lax.fori_loop(0, GX, gather, 0)

    def sweep(t, edge, first, start_re, start_im):
        at = 4 if edge else t
        inv = [(alpha[at, first + d, 0], alpha[at, first + d, 1]) for d in range(6)]

        def cells(step, psi):
            src = (GX - 1 - step) if first == 0 else step
            psi = list(psi)
            for zz in (1, 0) if first == 0 else (0, 1):
                z = 2 * src + zz
                if edge:
                    s_re, s_im = espec[src, zz], espec[src, 2 + zz]
                    g = [jnp.where(upper, edge_goal[z, 2 * c : 2 * c + 1], edge_goal[z, 2 * c + 1 : 2 * c + 2]) for c in range(2)]
                else:
                    s_re, s_im = spec[src, zz * 4 + t], spec[src, 8 + zz * 4 + t]
                    g = [
                        jnp.where(upper, goal[z, c, pl.ds(2 * t, 1), :], goal[z, c, pl.ds(2 * t + 1, 1), :])
                        for c in range(2)
                    ]
                s_re, s_im = s_re * rate, s_im * rate
                sum_re = sum_im = None
                for d in range(6):
                    t_re = s_re + couple[d] * psi[2 * d]
                    t_im = s_im + couple[d] * psi[2 * d + 1]
                    p_re = inv[d][0] * t_re - inv[d][1] * t_im
                    p_im = inv[d][0] * t_im + inv[d][1] * t_re
                    psi[2 * d], psi[2 * d + 1] = p_re, p_im
                    sum_re = p_re if d == 0 else sum_re + p_re
                    sum_im = p_im if d == 0 else sum_im + p_im
                    acc[z, first + d] += p_re * g[0] + p_im * g[1]
                if first == 0:
                    if edge:
                        enew[src, zz], enew[src, 2 + zz] = sum_re, sum_im
                    else:
                        back[src, zz * 4 + t], back[src, 8 + zz * 4 + t] = sum_re, sum_im
                elif not edge:
                    back[src, zz * 4 + t] = (back[src, zz * 4 + t] + sum_re) * (1.0 / 12.0)
                    back[src, 8 + zz * 4 + t] = (back[src, 8 + zz * 4 + t] + sum_im) * (1.0 / 12.0)
                else:
                    close(src, zz, (enew[src, zz] + sum_re) * (1.0 / 12.0), (enew[src, 2 + zz] + sum_im) * (1.0 / 12.0))
            return tuple(psi)

        return lax.fori_loop(0, GX, cells, tuple([start_re, start_im] * 6))

    mean = jnp.where(upper & (gx == HALF // ROWS), 0.5, 0.0)

    def close(src, zz, e_re, e_im):
        packed = []
        for c, e in ((0, e_re), (1, e_im)):
            at = 8 * c + zz * 4
            first = back[src, at]
            back[src, at] = first + mean * (pltpu.roll(e, 4, 0) - first)
            h = 0.5 * (e + pltpu.roll(e, HALF - 8, 1))
            packed.append(jnp.where(upper, h, pltpu.roll(pltpu.roll(h, 4, 0), HALF - 1, 1)))
        for t in range(4):
            x_re, x_im = [jnp.where(lane == 0, v if t == 0 else pltpu.roll(v, HALF - 2 * t, 1), 0.0) for v in packed]
            back[src, zz * 4 + t] = back[src, zz * 4 + t] - x_im
            back[src, 8 + zz * 4 + t] = back[src, 8 + zz * 4 + t] + x_re

    def absorbed(psi):
        parts = []
        for c in range(2):
            total = psi[c] * float(abs(COS[0]) / 12.0)
            for d in range(1, 6):
                total = total + psi[2 * d + c] * float(abs(COS[d]) / 12.0)
            parts.append(total)
        return parts

    zero = jnp.zeros((ROWS, HALF), jnp.float32)

    def down(t, carry):
        flux[2 * t], flux[2 * t + 1] = absorbed(sweep(t, False, 0, zero, zero))
        return carry

    flux[8], flux[9] = absorbed(sweep(0, True, 0, zero, zero))
    lax.fori_loop(0, 4, down, 0)

    pl.semaphore_wait(barrier, BA - 1)
    copies = []
    for k in range(1, BA):
        copies.append(
            pltpu.make_async_remote_copy(
                src_ref=flux,
                dst_ref=others.at[k - 1],
                send_sem=send.at[k - 1],
                recv_sem=recv.at[k - 1],
                device_id=(gx, lax.rem(ba + k, BA)),
                device_id_type=MESH,
            )
        )
        copies[-1].start()
    for copy in copies:
        copy.wait()

    odd, second = sub % 2 == 1, sub % 4 >= 2

    def wall(at):
        total = flux[at] + others[0, at] + others[1, at] + others[2, at]
        total = total + jnp.where(odd, pltpu.roll(total, 1, 0), pltpu.roll(total, ROWS - 1, 0))
        total = total + jnp.where(second, pltpu.roll(total, 2, 0), pltpu.roll(total, ROWS - 2, 0))
        return total * share

    def up(t, carry):
        sweep(t, False, 6, wall(2 * t), wall(2 * t + 1))
        return carry

    lax.fori_loop(0, 4, up, 0)
    sweep(0, True, 6, wall(8), wall(9))

    def reduce(src, carry):
        tile = jnp.zeros((ROWS, HALF), jnp.float32)
        for zz in range(2):
            for d in range(12):
                total = jnp.sum(acc[2 * src + zz, d], axis=1, keepdims=True)
                tile = jnp.where(lane == zz * 12 + d, total, tile)
        grads[src] = tile * (1.0 / N)
        return carry

    lax.fori_loop(0, GX, reduce, 0)


def vmem(count):
    return [pl.BlockSpec(memory_space=pltpu.VMEM)] * count


def solve(spec, goal, edge_goal, alpha, bands):
    f32 = jnp.float32
    return pl.pallas_call(
        solve_kernel,
        out_shape=[jax.ShapeDtypeStruct((GX, 16, ROWS, HALF), f32), jax.ShapeDtypeStruct((GX, ROWS, HALF), f32)],
        in_specs=vmem(5),
        out_specs=vmem(2),
        scratch_shapes=[
            pltpu.VMEM((64, 12, ROWS, HALF), f32),
            pltpu.VMEM((GX, 4, ROWS, HALF), f32),
            pltpu.VMEM((GX, 4, ROWS, HALF), f32),
            pltpu.VMEM((10, ROWS, HALF), f32),
            pltpu.VMEM((3, 10, ROWS, HALF), f32),
            pltpu.SemaphoreType.DMA((3,)),
            pltpu.SemaphoreType.DMA((3,)),
        ],
        compiler_params=pltpu.CompilerParams(collective_id=5, has_side_effects=True, vmem_limit_bytes=40 << 20),
        name="solve",
    )(spec, goal, edge_goal, alpha, bands)


def forward_transform(phi, rows, cos, sin):
    return pl.pallas_call(
        forward_kernel,
        out_shape=jax.ShapeDtypeStruct((GX, 136, HALF), jnp.float32),
        in_specs=vmem(7),
        out_specs=vmem(1)[0],
        scratch_shapes=[pltpu.VMEM((ROWS, N), jnp.float32)],
        compiler_params=pltpu.CompilerParams(vmem_limit_bytes=40 << 20),
        name="transform",
    )(phi, *rows, *cos, *sin)


def inverse_transform(back, coeff, rows, cos, sin):
    return pl.pallas_call(
        inverse_kernel,
        out_shape=jax.ShapeDtypeStruct((2, 4, N, N), jnp.float32),
        in_specs=vmem(8),
        out_specs=vmem(1)[0],
        compiler_params=pltpu.CompilerParams(vmem_limit_bytes=40 << 20),
        name="inverse",
    )(back, coeff, *rows, *cos, *sin)


def signed(index):
    return ((index + HALF) % N - HALF).astype(jnp.float32) * BASE


def propagators(rates, speeds, gx):
    sub = jnp.arange(ROWS)[:, None]
    lane = jnp.arange(HALF)[None, :]
    rate, speed = jnp.tile(rates, 2)[:, None], jnp.tile(speeds, 2)[:, None]
    fx, fy = [], []
    for t in range(4):
        fx.append(jnp.broadcast_to(signed(gx * ROWS + 2 * t + sub // 4), (ROWS, HALF)))
        fy.append(jnp.broadcast_to(signed(lane), (ROWS, HALF)))
    kx = gx * ROWS + lane % ROWS
    line = signed(kx)
    line = jnp.where((lane >= 8) & (kx == HALF), -line, line)
    fx.append(jnp.where(sub < 4, line, HALF * BASE))
    fy.append(jnp.where(sub < 4, jnp.where(lane < 8, -HALF * BASE, HALF * BASE), signed(lane)))
    fx, fy = jnp.stack(fx)[:, None], jnp.stack(fy)[:, None]
    sx, sy = jnp.asarray(SX, jnp.float32)[None, :, None, None], jnp.asarray(SY, jnp.float32)[None, :, None, None]
    wave = speed * (sx * fx + sy * fy)
    real = rate + jnp.asarray(np.abs(COS), jnp.float32)[None, :, None, None] * speed
    denom = real * real + wave * wave
    return jnp.stack([real / denom, -wave / denom], axis=2)


def targets(forward, gx):
    low = forward[..., :HALF]
    turned = jnp.flip(jnp.roll(forward, -1, axis=4)[..., HALF:], axis=4)
    ba_free = [(i, GX - 1 - i) for i in range(GX)]
    block = lax.ppermute(jnp.flip(jnp.roll(turned, -1, axis=3), axis=3), "gx", ba_free)
    lead = lax.ppermute(turned[:, :, :, :1], "gx", [(i, (GX - i) % GX) for i in range(GX)])
    mirror = jnp.concatenate([lead, block[:, :, :, 1:]], axis=3)
    lane = jnp.arange(HALF)[None, :]
    kx = gx * ROWS + jnp.arange(ROWS)[:, None]
    mirror = jnp.where((lane > 0) & (kx != HALF), mirror, 0.0)
    sign = jnp.array([1.0, -1.0], jnp.float32).reshape(1, 2, 1, 1, 1)
    goal = jnp.swapaxes(low + sign * mirror, 1, 2)
    own = jnp.where((lane > 0) & (gx == HALF // ROWS), turned[:, :, :, 0] * sign[..., 0], 0.0)
    line = jnp.pad(forward[..., HALF], ((0, 0), (0, 0), (0, 0), (0, HALF - ROWS)))
    edge = jnp.stack([line, own], axis=3)
    edge = jnp.swapaxes(edge, 1, 2).reshape(forward.shape[0], 64, 4, HALF)
    return goal, edge


def body(phi_start, coeff, forward, rates, speeds, shares):
    rows, inv_rows, cos, sin = tables()
    gx = lax.axis_index("gx")
    goal, edge = targets(forward, gx)
    alpha = propagators(rates, speeds, gx)
    bands = jnp.broadcast_to(jnp.tile(jnp.stack([rates, speeds, shares]), (1, 2))[:, :, None], (3, ROWS, HALF))
    phi = phi_start
    total = None
    for step in range(forward.shape[0]):
        spec = exchange(forward_transform(phi, rows, cos, sin), 1)
        back, grads = solve(spec.reshape(GX, 17, ROWS, HALF), goal[step], edge[step], alpha, bands)
        total = grads if step == 0 else total + grads
        back = exchange(back.reshape(GX, 128, HALF), 2)
        phi = inverse_transform(back, coeff, inv_rows, cos, sin)
    parts = jnp.sum(exchange(total, 3), axis=0)[:, :24].reshape(2, 4, 2, 12)
    return (phi, jnp.transpose(parts[0] + parts[1], (1, 2, 0)))


def solution(mesh):
    in_specs = (
        P("gx", "ba", None, None),
        P("gx", None, None),
        P(None, None, None, "gx", None),
        P("ba"),
        P("ba"),
        P("ba"),
    )
    out_specs = (P("gx", "ba", None, None), P("gx", None, "ba"))
    return jax.shard_map(body, mesh=mesh, in_specs=in_specs, out_specs=out_specs, check_vma=False)
```

```python
import functools
import math

import jax
import jax.numpy as jnp
import numpy as np
from jax import lax
from jax.experimental import pallas as pl
from jax.experimental.pallas import tpu as pltpu
from jax.sharding import PartitionSpec as P

MESH = pl.DeviceIdType.MESH
N = 256
HALF = 128
GX = 32
BA = 4
ROWS = 8
BASE = 1.5 * 2.0 * math.pi / N


def quadrature():
    level = np.arange(6)
    polar = 0.2 + 0.15 * level
    cosine = np.concatenate([-polar, polar])
    azimuth = np.concatenate([level * (math.pi / 3.0) + math.pi / 6.0, level * (math.pi / 3.0)])
    sine = np.sqrt(1.0 - cosine * cosine)
    return cosine, sine * np.cos(azimuth), sine * np.sin(azimuth)


COS, SX, SY = quadrature()


def halves(table):
    table = jnp.asarray(table, jnp.float32)
    high = table.astype(jnp.bfloat16)
    return high, (table - high.astype(jnp.float32)).astype(jnp.bfloat16)


def np_halves(table):
    table = np.asarray(table, np.float32)
    high = table.astype(jnp.bfloat16)
    low = (table - high.astype(np.float32)).astype(jnp.bfloat16)
    return [jnp.asarray(high), jnp.asarray(low)]


def tables():
    index = np.arange(N)
    angle = (index[:, None] * index[None, :] % N) * (2.0 * np.pi / N)
    cos, sin = np.cos(angle) / 16.0, np.sin(angle) / 16.0
    rows = np.concatenate([cos[:, :HALF], -sin[:, :HALF]], axis=1)
    rows[:, HALF] = cos[:, HALF]
    back = np.concatenate([2.0 * cos[:HALF], -2.0 * sin[:HALF]], axis=0)
    back[0] = cos[0]
    back[HALF] = cos[HALF]
    order = np.arange(N).reshape(GX, ROWS).T.reshape(-1)
    stacks = [rows, back, cos, sin, cos[order], sin[order], cos[:, order], sin[:, order]]
    return [part for stack in stacks for part in np_halves(stack)]


def split(value):
    high = value.astype(jnp.bfloat16)
    return high, (value - high.astype(jnp.float32)).astype(jnp.bfloat16)


def product(left, right):
    lh, ll = left
    rh, rl = right
    dot = functools.partial(jnp.dot, preferred_element_type=jnp.float32)
    return dot(lh, rh) + (dot(ll, rh) + dot(lh, rl))


SENT = 136
BACK = 128
OUTWARD = ((0, 2), (2, 3), (5, 4), (9, 4), (13, 4))
HOMEWARD = ((0, 4), (4, 4), (8, 4), (12, 4))
FLUXES = ((0, 4), (4, 2), (6, 2), (8, 2))
TABLES = 16


def spot(t, zz, part):
    return 4 * t + 2 * zz + part + (1 if t > 0 else 0)


def tile_of(ref, row):
    return ref[pl.ds(pl.multiple_of(row, ROWS), ROWS), :]


def kernel(phi, coeff_in, goal_in, edge_in, alpha, bands, *rest):
    names = [rest[2 * i : 2 * i + 2] for i in range(TABLES // 2)]
    wave_y, back_y, cos_x, sin_x, cos_rows, sin_rows, cos_cols, sin_cols = names
    (out, grads, field, coeff, goal, edge_goal, sent, spec, made, back, acc, espec, enew, epack, flux, others,
     gsum, gall, line_of, load, store, own, own_back, send, recv, send_back, recv_back, send_flux, recv_flux,
     send_grad, recv_grad) = rest[TABLES:]
    gx, ba = lax.axis_index("gx"), lax.axis_index("ba")
    barrier = pltpu.get_barrier_semaphore()

    def greet(k, carry):
        pl.semaphore_signal(barrier, inc=1, device_id=(lax.rem(gx + k, GX), ba), device_id_type=MESH)
        return carry

    lax.fori_loop(1, GX, greet, 0)
    for k in range(1, BA):
        pl.semaphore_signal(barrier, inc=1, device_id=(gx, lax.rem(ba + k, BA)), device_id_type=MESH)

    loads = [
        pltpu.make_async_copy(phi.at[0], field.at[0], load.at[0]),
        pltpu.make_async_copy(phi.at[1], field.at[1], load.at[1]),
        pltpu.make_async_copy(goal_in, goal, load.at[2]),
        pltpu.make_async_copy(edge_in, edge_goal, load.at[3]),
        pltpu.make_async_copy(coeff_in, coeff, load.at[4]),
    ]
    for copy in loads:
        copy.start()

    sub = lax.broadcasted_iota(jnp.int32, (ROWS, HALF), 0)
    lane = lax.broadcasted_iota(jnp.int32, (ROWS, HALF), 1)
    upper = sub < 4
    rate, speed, share = bands[0], bands[1], bands[2]
    couple = [speed * float(abs(COS[d])) for d in range(6)]
    zero = jnp.zeros((ROWS, HALF), jnp.float32)

    def clear(z, carry):
        for d in range(12):
            acc[z, d] = zero
        return carry

    lax.fori_loop(0, 64, clear, 0)

    def outward(message, k):
        first, count = OUTWARD[message]
        to = lax.rem(gx + k, GX)
        return pltpu.make_async_remote_copy(
            src_ref=sent.at[pl.ds(pl.multiple_of(to * SENT + first * ROWS, ROWS), count * ROWS), :],
            dst_ref=spec.at[pl.ds(pl.multiple_of(gx * SENT + first * ROWS, ROWS), count * ROWS), :],
            send_sem=send.at[message, k],
            recv_sem=recv.at[message, k],
            device_id=(to, ba),
            device_id_type=MESH,
        )

    def outward_own(message):
        first, count = OUTWARD[message]
        rows = pl.ds(pl.multiple_of(gx * SENT + first * ROWS, ROWS), count * ROWS)
        return pltpu.make_async_copy(sent.at[rows, :], spec.at[rows, :], own.at[message])

    def homeward(message, k):
        first, count = HOMEWARD[message]
        to = lax.rem(gx + k, GX)
        return pltpu.make_async_remote_copy(
            src_ref=made.at[pl.ds(pl.multiple_of(to * BACK + first * ROWS, ROWS), count * ROWS), :],
            dst_ref=back.at[pl.ds(pl.multiple_of(gx * BACK + first * ROWS, ROWS), count * ROWS), :],
            send_sem=send_back.at[message, k],
            recv_sem=recv_back.at[message, k],
            device_id=(to, ba),
            device_id_type=MESH,
        )

    def homeward_own(message):
        first, count = HOMEWARD[message]
        rows = pl.ds(pl.multiple_of(gx * BACK + first * ROWS, ROWS), count * ROWS)
        return pltpu.make_async_copy(made.at[rows, :], back.at[rows, :], own_back.at[message])

    def wall_copy(s, message, k):
        first, count = FLUXES[message]
        return pltpu.make_async_remote_copy(
            src_ref=flux.at[s, pl.ds(first, count)],
            dst_ref=others.at[s, k - 1, pl.ds(first, count)],
            send_sem=send_flux.at[s, message, k - 1],
            recv_sem=recv_flux.at[s, message, k - 1],
            device_id=(gx, lax.rem(ba + k, BA)),
            device_id_type=MESH,
        )

    def grad_copy(k):
        to = lax.rem(gx + k, GX)
        return pltpu.make_async_remote_copy(
            src_ref=gsum.at[to],
            dst_ref=gall.at[gx],
            send_sem=send_grad.at[k],
            recv_sem=recv_grad.at[k],
            device_id=(to, ba),
            device_id_type=MESH,
        )

    def over_peers(act):
        def one(k, carry):
            act(k)
            return carry

        lax.fori_loop(1, GX, one, 0)

    def start_outward(message):
        outward_own(message).start()
        over_peers(lambda k: outward(message, k).start())

    def wait_outward(message):
        outward_own(message).wait()
        over_peers(lambda k: outward(message, k).wait_recv())

    def start_homeward(message):
        homeward_own(message).start()
        over_peers(lambda k: homeward(message, k).start())

    def wait_homeward():
        for message in range(len(HOMEWARD)):
            homeward_own(message).wait()
            over_peers(lambda k: homeward(message, k).wait_recv())

    def sends_done(s):
        for message in range(len(OUTWARD)):
            over_peers(lambda k: outward(message, k).wait_send())
        for message in range(len(HOMEWARD)):
            over_peers(lambda k: homeward(message, k).wait_send())
        for message in range(len(FLUXES)):
            for k in range(1, BA):
                wall_copy(s, message, k).wait_send()

    inner = lax.broadcasted_iota(jnp.int32, (N, HALF), 1) != 0
    row8 = lax.broadcasted_iota(jnp.int32, (ROWS, N), 0)
    sign = jnp.where(lax.broadcasted_iota(jnp.int32, (ROWS, N), 1) % 2 == 0, 1.0 / 16.0, -1.0 / 16.0)

    def both(pair):
        return pair[0][...], pair[1][...]

    def forward(zz):
        def plane(b, carry):
            value = split(field[zz, b])
            rows = split(product(value, both(wave_y)))
            u = product(both(cos_rows), rows)
            v = product(both(sin_rows), rows)
            re = u[:, :HALF] + jnp.where(inner, v[:, HALF:], 0.0)
            im = jnp.where(inner, u[:, HALF:], 0.0) - v[:, :HALF]
            for t in range(4):
                for r in range(2):
                    for m in range(0, GX, ROWS):
                        at = (2 * t + r) * GX + m
                        for part, value_ in ((0, re), (1, im)):
                            row = m * SENT + spot(t, zz, part) * ROWS + r * 4
                            sent[pl.ds(row + b, ROWS, stride=SENT), :] = value_[at : at + ROWS]
            pick = jnp.where(row8 == zz * 4 + b, sign, 0.0).astype(jnp.bfloat16)
            nt = (((1,), (1,)), ((), ()))
            line_of[...] += lax.dot_general(
                pick, value[0], nt, preferred_element_type=jnp.float32
            ) + lax.dot_general(pick, value[1], nt, preferred_element_type=jnp.float32)
            return carry

        lax.fori_loop(0, 4, plane, 0)

    def edges():
        line = split(line_of[...])
        line_re = product(line, both(cos_x))
        line_im = -product(line, both(sin_x))
        for m in range(GX):
            at, off = HALF * (m // 16), 8 * (m % 16)
            re, im = line_re[:, at : at + HALF], line_im[:, at : at + HALF]
            tile = jnp.where(lane < 8, pltpu.roll(re, (HALF - off) % HALF, 1), 0.0)
            tile = jnp.where((lane >= 8) & (lane < 16), pltpu.roll(re, (HALF + 8 - off) % HALF, 1), tile)
            tile = jnp.where((lane >= 64) & (lane < 72), pltpu.roll(im, (HALF + 64 - off) % HALF, 1), tile)
            tile = jnp.where((lane >= 72) & (lane < 80), pltpu.roll(im, (HALF + 72 - off) % HALF, 1), tile)
            sent[m * SENT + 32 : m * SENT + 40, :] = tile

    def inverse(zz):
        def plane(b, carry):
            parts = []
            for part in range(2):
                pieces = []
                for t in range(4):
                    for r in range(2):
                        for m in range(0, GX, ROWS):
                            row = m * BACK + (4 * t + 2 * zz + part) * ROWS + r * 4
                            pieces.append(back[pl.ds(row + b, ROWS, stride=BACK), :])
                parts.append(jnp.concatenate(pieces, axis=0))
            modes = split(jnp.concatenate(parts, axis=1))
            u = product(both(cos_cols), modes)
            v = product(both(sin_cols), modes)
            rows = jnp.concatenate([u[:, :HALF] - v[:, HALF:], u[:, HALF:] + v[:, :HALF]], axis=1)
            field[zz, b] = product(split(rows), both(back_y)) * coeff[zz]
            return carry

        lax.fori_loop(0, 4, plane, 0)

    def gather():
        def one(src, carry):
            base = src * SENT
            line = tile_of(spec, base + 4 * ROWS)
            for zz in range(2):
                col = line if zz == 0 else pltpu.roll(line, 4, 0)
                col_re = jnp.where(lane < 16, col, 0.0)
                col_im = jnp.where(lane < 16, pltpu.roll(col, 64, 1), 0.0)
                espec[src, zz] = jnp.where(upper, col_re, pltpu.roll(tile_of(spec, base + spot(0, zz, 0) * ROWS), 4, 0))
                espec[src, 2 + zz] = jnp.where(
                    upper, col_im, pltpu.roll(tile_of(spec, base + spot(0, zz, 1) * ROWS), 4, 0)
                )
            return carry

        lax.fori_loop(0, GX, one, 0)

    mean = jnp.where(upper & (gx == HALF // ROWS), 0.5, 0.0)

    def sweep(s, t, first, start_re, start_im):
        edge = t == 4
        inv = [(alpha[t, first + d, 0], alpha[t, first + d, 1]) for d in range(6)]

        def cells(step, psi):
            src = (GX - 1 - step) if first == 0 else step
            psi = list(psi)
            for zz in (1, 0) if first == 0 else (0, 1):
                z = 2 * src + zz
                if edge:
                    s_re, s_im = espec[src, zz], espec[src, 2 + zz]
                    g = [
                        jnp.where(upper, edge_goal[s, z, 2 * c : 2 * c + 1], edge_goal[s, z, 2 * c + 1 : 2 * c + 2])
                        for c in range(2)
                    ]
                else:
                    s_re = tile_of(spec, src * SENT + spot(t, zz, 0) * ROWS)
                    s_im = tile_of(spec, src * SENT + spot(t, zz, 1) * ROWS)
                    g = [
                        jnp.where(upper, goal[s, z, c, 2 * t : 2 * t + 1], goal[s, z, c, 2 * t + 1 : 2 * t + 2])
                        for c in range(2)
                    ]
                s_re, s_im = s_re * rate, s_im * rate
                sums = [None, None]
                for d in range(6):
                    t_re = s_re + couple[d] * psi[2 * d]
                    t_im = s_im + couple[d] * psi[2 * d + 1]
                    p_re = inv[d][0] * t_re - inv[d][1] * t_im
                    p_im = inv[d][0] * t_im + inv[d][1] * t_re
                    psi[2 * d], psi[2 * d + 1] = p_re, p_im
                    sums = [p_re, p_im] if d == 0 else [sums[0] + p_re, sums[1] + p_im]
                    acc[z, first + d] += p_re * g[0] + p_im * g[1]
                if edge:
                    if first == 0:
                        enew[src, zz], enew[src, 2 + zz] = sums
                        continue
                    for c in range(2):
                        e = (enew[src, 2 * c + zz] + sums[c]) * (1.0 / 12.0)
                        enew[src, 2 * c + zz] = pltpu.roll(e, 4, 0)
                        h = 0.5 * (e + pltpu.roll(e, HALF - 8, 1))
                        epack[src, 2 * c + zz] = jnp.where(
                            upper, h, pltpu.roll(pltpu.roll(h, 4, 0), HALF - 1, 1)
                        )
                    continue
                for c in range(2):
                    rows = pl.ds(pl.multiple_of(src * BACK + (4 * t + 2 * zz + c) * ROWS, ROWS), ROWS)
                    if first == 0:
                        made[rows, :] = sums[c]
                        continue
                    total = (made[rows, :] + sums[c]) * (1.0 / 12.0)
                    if t == 0:
                        total = total + mean * (enew[src, 2 * c + zz] - total)
                    x = epack[src, 2 * (1 - c) + zz]
                    x = jnp.where(lane == 0, x if t == 0 else pltpu.roll(x, HALF - 2 * t, 1), 0.0)
                    made[rows, :] = total - x if c == 0 else total + x
            return tuple(psi)

        return lax.fori_loop(0, GX, cells, tuple([start_re, start_im] * 6))

    def down(s, t):
        psi = sweep(s, t, 0, zero, zero)
        at = 0 if t == 4 else 2 * t + 2
        for c in range(2):
            total = psi[c] * float(abs(COS[0]) / 12.0)
            for d in range(1, 6):
                total = total + psi[2 * d + c] * float(abs(COS[d]) / 12.0)
            flux[s, at + c] = total

    odd, second = sub % 2 == 1, sub % 4 >= 2

    def up(s, t):
        at = 0 if t == 4 else 2 * t + 2
        starts = []
        for c in range(2):
            total = flux[s, at + c] + others[s, 0, at + c] + others[s, 1, at + c] + others[s, 2, at + c]
            total = total + jnp.where(odd, pltpu.roll(total, 1, 0), pltpu.roll(total, ROWS - 1, 0))
            total = total + jnp.where(second, pltpu.roll(total, 2, 0), pltpu.roll(total, ROWS - 2, 0))
            starts.append(total * share)
        sweep(s, t, 6, *starts)

    def start_wall(s, message):
        for k in range(1, BA):
            wall_copy(s, message, k).start()

    def wait_wall(s, message):
        for k in range(1, BA):
            wall_copy(s, message, k).wait_recv()

    def one_step(s, carry):
        line_of[...] = jnp.zeros_like(line_of)

        @pl.when(s > 0)
        def _():
            wait_homeward()
            sends_done(s - 1)
            inverse(0)

        @pl.when(s == 0)
        def _():
            loads[0].wait()

        forward(0)

        @pl.when(s == 0)
        def _():
            pl.semaphore_wait(barrier, GX - 1 + BA - 1)

        start_outward(0)

        @pl.when(s > 0)
        def _():
            inverse(1)

        @pl.when(s == 0)
        def _():
            loads[1].wait()

        forward(1)
        edges()
        for message in range(1, len(OUTWARD)):
            start_outward(message)

        @pl.when(s == 0)
        def _():
            for copy in loads[2:]:
                copy.wait()

        wait_outward(0)
        wait_outward(1)
        gather()
        down(s, 4)
        down(s, 0)
        start_wall(s, 0)
        wait_outward(2)
        down(s, 1)
        start_wall(s, 1)
        wait_wall(s, 0)
        up(s, 4)
        up(s, 0)
        start_homeward(0)
        for t in (1, 2):
            wait_outward(t + 2)
            down(s, t + 1)
            start_wall(s, t + 1)
            wait_wall(s, t)
            up(s, t)
            start_homeward(t)
        wait_wall(s, 3)
        up(s, 3)
        start_homeward(3)
        return carry

    lax.fori_loop(0, 2, one_step, 0)

    def reduce(src, carry):
        tile = zero
        for zz in range(2):
            for d in range(12):
                total = jnp.sum(acc[2 * src + zz, d], axis=1, keepdims=True)
                tile = jnp.where(lane == zz * 12 + d, total, tile)
        gsum[src] = tile * (1.0 / N)
        return carry

    lax.fori_loop(0, GX, reduce, 0)
    over_peers(lambda k: grad_copy(k).start())
    wait_homeward()
    stores = [pltpu.make_async_copy(field.at[zz], out.at[zz], store.at[zz]) for zz in range(2)]
    for zz in range(2):
        inverse(zz)
        stores[zz].start()
    over_peers(lambda k: grad_copy(k).wait())
    gall[gx] = gsum[gx]
    total = gall[0]
    for src in range(1, GX):
        total = total + gall[src]
    grads[...] = total
    sends_done(1)
    for copy in stores:
        copy.wait()


def program(phi, coeff, goal, edge, alpha, bands):
    f32 = jnp.float32
    dma = pltpu.SemaphoreType.DMA
    tile = (ROWS, HALF)
    hbm, local = pl.BlockSpec(memory_space=pl.ANY), pl.BlockSpec(memory_space=pltpu.VMEM)
    return pl.pallas_call(
        kernel,
        out_shape=[jax.ShapeDtypeStruct((2, 4, N, N), f32), jax.ShapeDtypeStruct(tile, f32)],
        in_specs=[hbm] * 4 + [local] * (2 + TABLES),
        out_specs=[hbm, local],
        scratch_shapes=[
            pltpu.VMEM((2, 4, N, N), f32),
            pltpu.VMEM((2, N, N), f32),
            pltpu.VMEM((2, 64, 2) + tile, f32),
            pltpu.VMEM((2, 64, 4, HALF), f32),
            pltpu.VMEM((GX * SENT, HALF), f32),
            pltpu.VMEM((GX * SENT, HALF), f32),
            pltpu.VMEM((GX * BACK, HALF), f32),
            pltpu.VMEM((GX * BACK, HALF), f32),
            pltpu.VMEM((64, 12) + tile, f32),
            pltpu.VMEM((GX, 4) + tile, f32),
            pltpu.VMEM((GX, 4) + tile, f32),
            pltpu.VMEM((GX, 4) + tile, f32),
            pltpu.VMEM((2, 10) + tile, f32),
            pltpu.VMEM((2, 3, 10) + tile, f32),
            pltpu.VMEM((GX,) + tile, f32),
            pltpu.VMEM((GX,) + tile, f32),
            pltpu.VMEM((ROWS, N), f32),
            dma((5,)),
            dma((2,)),
            dma((len(OUTWARD),)),
            dma((len(HOMEWARD),)),
            dma((len(OUTWARD), GX)),
            dma((len(OUTWARD), GX)),
            dma((len(HOMEWARD), GX)),
            dma((len(HOMEWARD), GX)),
            dma((2, len(FLUXES), BA - 1)),
            dma((2, len(FLUXES), BA - 1)),
            dma((GX,)),
            dma((GX,)),
        ],
        compiler_params=pltpu.CompilerParams(collective_id=0, has_side_effects=True, vmem_limit_bytes=56 << 20),
        name="transport",
    )(phi, coeff, goal, edge, alpha, bands, *tables())


def signed(index):
    return ((index + HALF) % N - HALF).astype(jnp.float32) * BASE


def propagators(rates, speeds, gx):
    sub = jnp.arange(ROWS)[:, None]
    lane = jnp.arange(HALF)[None, :]
    rate, speed = jnp.tile(rates, 2)[:, None], jnp.tile(speeds, 2)[:, None]
    fx, fy = [], []
    for t in range(4):
        fx.append(jnp.broadcast_to(signed(gx * ROWS + 2 * t + sub // 4), (ROWS, HALF)))
        fy.append(jnp.broadcast_to(signed(lane), (ROWS, HALF)))
    kx = gx * ROWS + lane % ROWS
    line = signed(kx)
    line = jnp.where((lane >= 8) & (kx == HALF), -line, line)
    fx.append(jnp.where(sub < 4, line, HALF * BASE))
    fy.append(jnp.where(sub < 4, jnp.where(lane < 8, -HALF * BASE, HALF * BASE), signed(lane)))
    fx, fy = jnp.stack(fx)[:, None], jnp.stack(fy)[:, None]
    sx, sy = jnp.asarray(SX, jnp.float32)[None, :, None, None], jnp.asarray(SY, jnp.float32)[None, :, None, None]
    wave = speed * (sx * fx + sy * fy)
    real = rate + jnp.asarray(np.abs(COS), jnp.float32)[None, :, None, None] * speed
    denom = real * real + wave * wave
    return jnp.stack([real / denom, -wave / denom], axis=2)


def targets(forward, gx):
    low = forward[..., :HALF]
    turned = jnp.flip(jnp.roll(forward, -1, axis=4)[..., HALF:], axis=4)
    ba_free = [(i, GX - 1 - i) for i in range(GX)]
    block = lax.ppermute(jnp.flip(jnp.roll(turned, -1, axis=3), axis=3), "gx", ba_free)
    lead = lax.ppermute(turned[:, :, :, :1], "gx", [(i, (GX - i) % GX) for i in range(GX)])
    mirror = jnp.concatenate([lead, block[:, :, :, 1:]], axis=3)
    lane = jnp.arange(HALF)[None, :]
    kx = gx * ROWS + jnp.arange(ROWS)[:, None]
    mirror = jnp.where((lane > 0) & (kx != HALF), mirror, 0.0)
    sign = jnp.array([1.0, -1.0], jnp.float32).reshape(1, 2, 1, 1, 1)
    goal = jnp.swapaxes(low + sign * mirror, 1, 2)
    own = jnp.where((lane > 0) & (gx == HALF // ROWS), turned[:, :, :, 0] * sign[..., 0], 0.0)
    line = jnp.pad(forward[..., HALF], ((0, 0), (0, 0), (0, 0), (0, HALF - ROWS)))
    edge = jnp.stack([line, own], axis=3)
    edge = jnp.swapaxes(edge, 1, 2).reshape(forward.shape[0], 64, 4, HALF)
    return goal, edge


def body(phi_start, coeff, forward, rates, speeds, shares):
    gx = lax.axis_index("gx")
    goal, edge = targets(forward, gx)
    alpha = propagators(rates, speeds, gx)
    bands = jnp.broadcast_to(jnp.tile(jnp.stack([rates, speeds, shares]), (1, 2))[:, :, None], (3, ROWS, HALF))
    phi, sums = program(phi_start, coeff, goal, edge, alpha, bands)
    parts = sums[:, :24].reshape(2, 4, 2, 12)
    return (phi, jnp.transpose(parts[0] + parts[1], (1, 2, 0)))


def solution(mesh):
    in_specs = (
        P("gx", "ba", None, None),
        P("gx", None, None),
        P(None, None, None, "gx", None),
        P("ba"),
        P("ba"),
        P("ba"),
    )
    out_specs = (P("gx", "ba", None, None), P("gx", None, "ba"))
    return jax.shard_map(body, mesh=mesh, in_specs=in_specs, out_specs=out_specs, check_vma=False)
```

```python
import functools
import math

import jax
import jax.numpy as jnp
import numpy as np
from jax import lax
from jax.experimental import pallas as pl
from jax.experimental.pallas import tpu as pltpu
from jax.sharding import PartitionSpec as P

MESH = pl.DeviceIdType.MESH
N = 256
HALF = 128
GX = 32
BA = 4
ROWS = 8
BASE = 1.5 * 2.0 * math.pi / N


def quadrature():
    level = np.arange(6)
    polar = 0.2 + 0.15 * level
    cosine = np.concatenate([-polar, polar])
    azimuth = np.concatenate([level * (math.pi / 3.0) + math.pi / 6.0, level * (math.pi / 3.0)])
    sine = np.sqrt(1.0 - cosine * cosine)
    return cosine, sine * np.cos(azimuth), sine * np.sin(azimuth)


COS, SX, SY = quadrature()


def halves(table):
    table = jnp.asarray(table, jnp.float32)
    high = table.astype(jnp.bfloat16)
    return high, (table - high.astype(jnp.float32)).astype(jnp.bfloat16)


def np_halves(table):
    table = np.asarray(table, np.float32)
    high = table.astype(jnp.bfloat16)
    low = (table - high.astype(np.float32)).astype(jnp.bfloat16)
    return [jnp.asarray(high), jnp.asarray(low)]


def tables():
    index = np.arange(N)
    angle = (index[:, None] * index[None, :] % N) * (2.0 * np.pi / N)
    cos, sin = np.cos(angle) / 16.0, np.sin(angle) / 16.0
    rows = np.concatenate([cos[:, :HALF], -sin[:, :HALF]], axis=1)
    rows[:, HALF] = cos[:, HALF]
    back = np.concatenate([2.0 * cos[:HALF], -2.0 * sin[:HALF]], axis=0)
    back[0] = cos[0]
    back[HALF] = cos[HALF]
    order = np.arange(N).reshape(GX, ROWS).T.reshape(-1)
    stacks = [rows, back, cos, sin, cos[order], sin[order], cos[:, order], sin[:, order]]
    return [part for stack in stacks for part in np_halves(stack)]


def split(value):
    high = value.astype(jnp.bfloat16)
    return high, (value - high.astype(jnp.float32)).astype(jnp.bfloat16)


def product(left, right):
    lh, ll = left
    rh, rl = right
    dot = functools.partial(jnp.dot, preferred_element_type=jnp.float32)
    return dot(lh, rh) + (dot(ll, rh) + dot(lh, rl))


SENT = 136
BACK = 128
OUTWARD = ((0, 2), (2, 3), (5, 4), (9, 4), (13, 4))
HOMEWARD = ((0, 4), (4, 4), (8, 4), (12, 4))
FLUXES = ((0, 4), (4, 2), (6, 2), (8, 2))
TABLES = 16


def spot(t, zz, part):
    return 4 * t + 2 * zz + part + (1 if t > 0 else 0)


def tile_of(ref, row):
    return ref[pl.ds(pl.multiple_of(row, ROWS), ROWS), :]


def kernel(phi, coeff_in, target, rates, speeds, shares, *rest):
    names = [rest[2 * i : 2 * i + 2] for i in range(TABLES // 2)]
    wave_y, back_y, cos_x, sin_x, cos_rows, sin_rows, cos_cols, sin_cols = names
    (field, grads, coeff, held, mirror, lead, lead_in, goal, edge_goal, alpha, sent, spec, made, back, acc, espec,
     enew, epack, flux, others, gsum, gall, line_of, load, own, own_back, send, recv, send_back, recv_back, send_flux,
     recv_flux, send_grad, recv_grad, send_turn, recv_turn, send_lead, recv_lead, send_share, recv_share) = rest[TABLES:]
    gx, ba = lax.axis_index("gx"), lax.axis_index("ba")
    barrier = pltpu.get_barrier_semaphore()

    def greet(k, carry):
        pl.semaphore_signal(barrier, inc=1, device_id=(lax.rem(gx + k, GX), ba), device_id_type=MESH)
        return carry

    lax.fori_loop(1, GX, greet, 0)
    for k in range(1, BA):
        pl.semaphore_signal(barrier, inc=1, device_id=(gx, lax.rem(ba + k, BA)), device_id_type=MESH)

    loads = [
        pltpu.make_async_copy(phi.at[0], field.at[0], load.at[0]),
        pltpu.make_async_copy(phi.at[1], field.at[1], load.at[1]),
        pltpu.make_async_copy(target, held, load.at[2]),
        pltpu.make_async_copy(coeff_in, coeff, load.at[3]),
    ]
    for copy in loads:
        copy.start()

    sub = lax.broadcasted_iota(jnp.int32, (ROWS, HALF), 0)
    lane = lax.broadcasted_iota(jnp.int32, (ROWS, HALF), 1)
    upper = sub < 4

    def by_band(values):
        spread = jnp.where(sub % 4 == 0, values[0], values[1])
        return jnp.where(sub % 4 >= 2, jnp.where(sub % 4 == 2, values[2], values[3]), spread)

    rate, speed, share = by_band(rates), by_band(speeds), by_band(shares)
    couple = [speed * float(abs(COS[d])) for d in range(6)]
    zero = jnp.zeros((ROWS, HALF), jnp.float32)

    def clear(z, carry):
        for d in range(12):
            acc[z, d] = zero
        return carry

    lax.fori_loop(0, 64, clear, 0)

    def signed(index):
        return (lax.rem(index + HALF, N) - HALF).astype(jnp.float32) * BASE

    def propagators():
        for t in range(5):
            if t < 4:
                fx, fy = signed(gx * ROWS + 2 * t + sub // 4), signed(lane)
            else:
                kx = gx * ROWS + lane % ROWS
                line = signed(kx)
                line = jnp.where((lane >= 8) & (kx == HALF), -line, line)
                fx = jnp.where(upper, line, HALF * BASE)
                fy = jnp.where(upper, jnp.where(lane < 8, -HALF * BASE, HALF * BASE), signed(lane))
            for d in range(12):
                wave = speed * (fx * float(SX[d]) + fy * float(SY[d]))
                real = rate + speed * float(abs(COS[d]))
                denom = real * real + wave * wave
                alpha[t, d, 0] = real / denom
                alpha[t, d, 1] = -wave / denom

    partner, first_row = GX - 1 - gx, lax.rem(GX - gx, GX)
    quarter = pl.ds(pl.multiple_of(ba * 16, 16), 16)

    def turn_copy(s):
        return pltpu.make_async_remote_copy(
            src_ref=held.at[s, :, quarter, :, pl.ds(HALF, HALF)],
            dst_ref=mirror.at[s, :, quarter],
            send_sem=send_turn.at[s],
            recv_sem=recv_turn.at[s],
            device_id=(partner, ba),
            device_id_type=MESH,
        )

    def share_copy(s, k):
        return pltpu.make_async_remote_copy(
            src_ref=mirror.at[s, :, quarter],
            dst_ref=mirror.at[s, :, quarter],
            send_sem=send_share.at[s, k - 1],
            recv_sem=recv_share.at[s, k - 1],
            device_id=(gx, lax.rem(ba + k, BA)),
            device_id_type=MESH,
        )

    def lead_copy(s):
        return pltpu.make_async_remote_copy(
            src_ref=lead.at[s],
            dst_ref=lead_in.at[s],
            send_sem=send_lead.at[s],
            recv_sem=recv_lead.at[s],
            device_id=(first_row, ba),
            device_id_type=MESH,
        )

    def lead_rows(s):
        for c in range(2):
            def one(z, carry):
                lead[s, c, pl.ds(z, 1), :] = held[s, c, z, 0:1, HALF:]
                return carry

            lax.fori_loop(0, 64, one, 0)

    def start_turn(s):
        turn_copy(s).start()

        @pl.when(first_row != gx)
        def _():
            lead_copy(s).start()

    def start_share(s):
        turn_copy(s).wait_recv()
        for k in range(1, BA):
            share_copy(s, k).start()

    def fold(s):
        for k in range(1, BA):
            share_copy(s, k).wait_recv()

        @pl.when(first_row != gx)
        def _():
            lead_copy(s).wait_recv()

        @pl.when(first_row == gx)
        def _():
            lead_in[s] = lead[s]

        lanes = lax.rem(HALF - lane, HALF)
        rows = lax.rem(ROWS - sub, ROWS)
        keep = (lane > 0) & ((gx != HALF // ROWS) | (sub > 0))
        alone = (lane > 0) & (gx == HALF // ROWS)

        def cell(z, carry):
            for c in range(2):
                tile = jnp.where(sub == 0, lead_in[s, c, pl.ds(z, 1), :], mirror[s, c, z])
                tile = jnp.take_along_axis(jnp.take_along_axis(tile, lanes, axis=1), rows, axis=0)
                tile = jnp.where(keep, tile, 0.0)
                low, high = held[s, c, z, :, :HALF], held[s, c, z, :, HALF:]
                goal[z, c] = low + tile if c == 0 else low - tile
                line = jnp.sum(jnp.where(lane == sub, jnp.broadcast_to(high[:, 0:1], (ROWS, HALF)), 0.0), axis=0, keepdims=True)
                other = jnp.where(alone, jnp.take_along_axis(high, lanes, axis=1), 0.0)
                other = other[0:1] if c == 0 else -other[0:1]
                edge_goal[z, c] = jnp.where(upper, line, other)
            return carry

        lax.fori_loop(0, 64, cell, 0)

    def turns_done():
        for s in range(2):
            turn_copy(s).wait_send()
            for k in range(1, BA):
                share_copy(s, k).wait_send()

            @pl.when(first_row != gx)
            def _():
                lead_copy(s).wait_send()

    def outward(message, k):
        first, count = OUTWARD[message]
        to = lax.rem(gx + k, GX)
        return pltpu.make_async_remote_copy(
            src_ref=sent.at[pl.ds(pl.multiple_of(to * SENT + first * ROWS, ROWS), count * ROWS), :],
            dst_ref=spec.at[pl.ds(pl.multiple_of(gx * SENT + first * ROWS, ROWS), count * ROWS), :],
            send_sem=send.at[message, k],
            recv_sem=recv.at[message, k],
            device_id=(to, ba),
            device_id_type=MESH,
        )

    def outward_own(message):
        first, count = OUTWARD[message]
        rows = pl.ds(pl.multiple_of(gx * SENT + first * ROWS, ROWS), count * ROWS)
        return pltpu.make_async_copy(sent.at[rows, :], spec.at[rows, :], own.at[message])

    def homeward(message, k):
        first, count = HOMEWARD[message]
        to = lax.rem(gx + k, GX)
        return pltpu.make_async_remote_copy(
            src_ref=made.at[pl.ds(pl.multiple_of(to * BACK + first * ROWS, ROWS), count * ROWS), :],
            dst_ref=back.at[pl.ds(pl.multiple_of(gx * BACK + first * ROWS, ROWS), count * ROWS), :],
            send_sem=send_back.at[message, k],
            recv_sem=recv_back.at[message, k],
            device_id=(to, ba),
            device_id_type=MESH,
        )

    def homeward_own(message):
        first, count = HOMEWARD[message]
        rows = pl.ds(pl.multiple_of(gx * BACK + first * ROWS, ROWS), count * ROWS)
        return pltpu.make_async_copy(made.at[rows, :], back.at[rows, :], own_back.at[message])

    def wall_copy(s, message, k):
        first, count = FLUXES[message]
        return pltpu.make_async_remote_copy(
            src_ref=flux.at[s, pl.ds(first, count)],
            dst_ref=others.at[s, k - 1, pl.ds(first, count)],
            send_sem=send_flux.at[s, message, k - 1],
            recv_sem=recv_flux.at[s, message, k - 1],
            device_id=(gx, lax.rem(ba + k, BA)),
            device_id_type=MESH,
        )

    def grad_copy(k):
        to = lax.rem(gx + k, GX)
        return pltpu.make_async_remote_copy(
            src_ref=gsum.at[to],
            dst_ref=gall.at[gx],
            send_sem=send_grad.at[k],
            recv_sem=recv_grad.at[k],
            device_id=(to, ba),
            device_id_type=MESH,
        )

    def over_peers(act):
        def one(k, carry):
            act(k)
            return carry

        lax.fori_loop(1, GX, one, 0)

    def start_outward(message):
        outward_own(message).start()
        over_peers(lambda k: outward(message, k).start())

    def wait_outward(message):
        outward_own(message).wait()
        over_peers(lambda k: outward(message, k).wait_recv())

    def start_homeward(message):
        homeward_own(message).start()
        over_peers(lambda k: homeward(message, k).start())

    def wait_homeward():
        for message in range(len(HOMEWARD)):
            homeward_own(message).wait()
            over_peers(lambda k: homeward(message, k).wait_recv())

    def sends_done(s):
        for message in range(len(OUTWARD)):
            over_peers(lambda k: outward(message, k).wait_send())
        for message in range(len(HOMEWARD)):
            over_peers(lambda k: homeward(message, k).wait_send())
        for message in range(len(FLUXES)):
            for k in range(1, BA):
                wall_copy(s, message, k).wait_send()

    inner = lax.broadcasted_iota(jnp.int32, (N, HALF), 1) != 0
    row8 = lax.broadcasted_iota(jnp.int32, (ROWS, N), 0)
    sign = jnp.where(lax.broadcasted_iota(jnp.int32, (ROWS, N), 1) % 2 == 0, 1.0 / 16.0, -1.0 / 16.0)

    def both(pair):
        return pair[0][...], pair[1][...]

    def forward(zz):
        def plane(b, carry):
            value = split(field[zz, b])
            rows = split(product(value, both(wave_y)))
            u = product(both(cos_rows), rows)
            v = product(both(sin_rows), rows)
            re = u[:, :HALF] + jnp.where(inner, v[:, HALF:], 0.0)
            im = jnp.where(inner, u[:, HALF:], 0.0) - v[:, :HALF]
            for t in range(4):
                for r in range(2):
                    for m in range(0, GX, ROWS):
                        at = (2 * t + r) * GX + m
                        for part, value_ in ((0, re), (1, im)):
                            row = m * SENT + spot(t, zz, part) * ROWS + r * 4
                            sent[pl.ds(row + b, ROWS, stride=SENT), :] = value_[at : at + ROWS]
            pick = jnp.where(row8 == zz * 4 + b, sign, 0.0).astype(jnp.bfloat16)
            nt = (((1,), (1,)), ((), ()))
            line_of[...] += lax.dot_general(
                pick, value[0], nt, preferred_element_type=jnp.float32
            ) + lax.dot_general(pick, value[1], nt, preferred_element_type=jnp.float32)
            return carry

        lax.fori_loop(0, 4, plane, 0)

    def edges():
        line = split(line_of[...])
        line_re = product(line, both(cos_x))
        line_im = -product(line, both(sin_x))
        for m in range(GX):
            at, off = HALF * (m // 16), 8 * (m % 16)
            re, im = line_re[:, at : at + HALF], line_im[:, at : at + HALF]
            tile = jnp.where(lane < 8, pltpu.roll(re, (HALF - off) % HALF, 1), 0.0)
            tile = jnp.where((lane >= 8) & (lane < 16), pltpu.roll(re, (HALF + 8 - off) % HALF, 1), tile)
            tile = jnp.where((lane >= 64) & (lane < 72), pltpu.roll(im, (HALF + 64 - off) % HALF, 1), tile)
            tile = jnp.where((lane >= 72) & (lane < 80), pltpu.roll(im, (HALF + 72 - off) % HALF, 1), tile)
            sent[m * SENT + 32 : m * SENT + 40, :] = tile

    def inverse(zz, last):
        def plane(b, carry):
            parts = []
            for part in range(2):
                pieces = []
                for t in range(4):
                    for r in range(2):
                        for m in range(0, GX, ROWS):
                            row = m * BACK + (4 * t + 2 * zz + part) * ROWS + r * 4
                            pieces.append(back[pl.ds(row + b, ROWS, stride=BACK), :])
                parts.append(jnp.concatenate(pieces, axis=0))
            modes = split(jnp.concatenate(parts, axis=1))
            u = product(both(cos_cols), modes)
            v = product(both(sin_cols), modes)
            rows = jnp.concatenate([u[:, :HALF] - v[:, HALF:], u[:, HALF:] + v[:, :HALF]], axis=1)
            value = product(split(rows), both(back_y))
            field[zz, b] = value if last else value * coeff[zz]
            return carry

        lax.fori_loop(0, 4, plane, 0)

    def gather():
        def one(src, carry):
            base = src * SENT
            line = tile_of(spec, base + 4 * ROWS)
            for zz in range(2):
                col = line if zz == 0 else pltpu.roll(line, 4, 0)
                col_re = jnp.where(lane < 16, col, 0.0)
                col_im = jnp.where(lane < 16, pltpu.roll(col, 64, 1), 0.0)
                espec[src, zz] = jnp.where(upper, col_re, pltpu.roll(tile_of(spec, base + spot(0, zz, 0) * ROWS), 4, 0))
                espec[src, 2 + zz] = jnp.where(
                    upper, col_im, pltpu.roll(tile_of(spec, base + spot(0, zz, 1) * ROWS), 4, 0)
                )
            return carry

        lax.fori_loop(0, GX, one, 0)

    mean = jnp.where(upper & (gx == HALF // ROWS), 0.5, 0.0)

    def sweep(s, t, first, start_re, start_im):
        edge = t == 4
        inv = [(alpha[t, first + d, 0], alpha[t, first + d, 1]) for d in range(6)]

        def cells(step, psi):
            src = (GX - 1 - step) if first == 0 else step
            psi = list(psi)
            for zz in (1, 0) if first == 0 else (0, 1):
                z = 2 * src + zz
                if edge:
                    s_re, s_im = espec[src, zz], espec[src, 2 + zz]
                    g = [edge_goal[z, c] for c in range(2)]
                else:
                    s_re = tile_of(spec, src * SENT + spot(t, zz, 0) * ROWS)
                    s_im = tile_of(spec, src * SENT + spot(t, zz, 1) * ROWS)
                    g = [
                        jnp.where(upper, goal[z, c, 2 * t : 2 * t + 1], goal[z, c, 2 * t + 1 : 2 * t + 2])
                        for c in range(2)
                    ]
                s_re, s_im = s_re * rate, s_im * rate
                sums = [None, None]
                for d in range(6):
                    t_re = s_re + couple[d] * psi[2 * d]
                    t_im = s_im + couple[d] * psi[2 * d + 1]
                    p_re = inv[d][0] * t_re - inv[d][1] * t_im
                    p_im = inv[d][0] * t_im + inv[d][1] * t_re
                    psi[2 * d], psi[2 * d + 1] = p_re, p_im
                    sums = [p_re, p_im] if d == 0 else [sums[0] + p_re, sums[1] + p_im]
                    acc[z, first + d] += p_re * g[0] + p_im * g[1]
                if edge:
                    if first == 0:
                        enew[src, zz], enew[src, 2 + zz] = sums
                        continue
                    for c in range(2):
                        e = (enew[src, 2 * c + zz] + sums[c]) * (1.0 / 12.0)
                        enew[src, 2 * c + zz] = pltpu.roll(e, 4, 0)
                        h = 0.5 * (e + pltpu.roll(e, HALF - 8, 1))
                        epack[src, 2 * c + zz] = jnp.where(
                            upper, h, pltpu.roll(pltpu.roll(h, 4, 0), HALF - 1, 1)
                        )
                    continue
                for c in range(2):
                    rows = pl.ds(pl.multiple_of(src * BACK + (4 * t + 2 * zz + c) * ROWS, ROWS), ROWS)
                    if first == 0:
                        made[rows, :] = sums[c]
                        continue
                    total = (made[rows, :] + sums[c]) * (1.0 / 12.0)
                    if t == 0:
                        total = total + mean * (enew[src, 2 * c + zz] - total)
                    x = epack[src, 2 * (1 - c) + zz]
                    x = jnp.where(lane == 0, x if t == 0 else pltpu.roll(x, HALF - 2 * t, 1), 0.0)
                    made[rows, :] = total - x if c == 0 else total + x
            return tuple(psi)

        return lax.fori_loop(0, GX, cells, tuple([start_re, start_im] * 6))

    def down(s, t):
        psi = sweep(s, t, 0, zero, zero)
        at = 0 if t == 4 else 2 * t + 2
        for c in range(2):
            total = psi[c] * float(abs(COS[0]) / 12.0)
            for d in range(1, 6):
                total = total + psi[2 * d + c] * float(abs(COS[d]) / 12.0)
            flux[s, at + c] = total

    odd, second = sub % 2 == 1, sub % 4 >= 2

    def up(s, t):
        at = 0 if t == 4 else 2 * t + 2
        starts = []
        for c in range(2):
            total = flux[s, at + c] + others[s, 0, at + c] + others[s, 1, at + c] + others[s, 2, at + c]
            total = total + jnp.where(odd, pltpu.roll(total, 1, 0), pltpu.roll(total, ROWS - 1, 0))
            total = total + jnp.where(second, pltpu.roll(total, 2, 0), pltpu.roll(total, ROWS - 2, 0))
            starts.append(total * share)
        sweep(s, t, 6, *starts)

    def start_wall(s, message):
        for k in range(1, BA):
            wall_copy(s, message, k).start()

    def wait_wall(s, message):
        for k in range(1, BA):
            wall_copy(s, message, k).wait_recv()

    def one_step(s, carry):
        line_of[...] = jnp.zeros_like(line_of)

        @pl.when(s > 0)
        def _():
            wait_homeward()
            sends_done(s - 1)
            inverse(0, False)

        @pl.when(s == 0)
        def _():
            loads[0].wait()

        forward(0)

        @pl.when(s == 0)
        def _():
            loads[2].wait()
            lead_rows(0)
            lead_rows(1)
            pl.semaphore_wait(barrier, GX - 1 + BA - 1)
            start_turn(0)

        start_outward(0)

        @pl.when(s > 0)
        def _():
            inverse(1, False)

        @pl.when(s == 0)
        def _():
            loads[1].wait()

        forward(1)
        edges()
        for message in range(1, len(OUTWARD)):
            start_outward(message)

        @pl.when(s == 0)
        def _():
            start_turn(1)
            start_share(0)
            propagators()
            loads[3].wait()

        fold(s)

        @pl.when(s == 0)
        def _():
            start_share(1)

        wait_outward(0)
        wait_outward(1)
        gather()
        down(s, 4)
        down(s, 0)
        start_wall(s, 0)
        wait_outward(2)
        down(s, 1)
        start_wall(s, 1)
        wait_wall(s, 0)
        up(s, 4)
        up(s, 0)
        start_homeward(0)
        for t in (1, 2):
            wait_outward(t + 2)
            down(s, t + 1)
            start_wall(s, t + 1)
            wait_wall(s, t)
            up(s, t)
            start_homeward(t)
        wait_wall(s, 3)
        up(s, 3)
        start_homeward(3)
        return carry

    lax.fori_loop(0, 2, one_step, 0)

    def reduce(src, carry):
        tile = zero
        for zz in range(2):
            for d in range(12):
                total = jnp.sum(acc[2 * src + zz, d], axis=1, keepdims=True)
                tile = jnp.where(lane == zz * 12 + d, total, tile)
        gsum[src] = tile * (1.0 / N)
        return carry

    lax.fori_loop(0, GX, reduce, 0)
    over_peers(lambda k: grad_copy(k).start())
    wait_homeward()
    for zz in range(2):
        inverse(zz, True)
    over_peers(lambda k: grad_copy(k).wait())
    gall[gx] = gsum[gx]
    total = gall[0]
    for src in range(1, GX):
        total = total + gall[src]
    grads[...] = total
    sends_done(1)
    turns_done()


def program(phi, coeff, target, rates, speeds, shares):
    f32 = jnp.float32
    dma = pltpu.SemaphoreType.DMA
    tile = (ROWS, HALF)
    hbm, local = pl.BlockSpec(memory_space=pl.ANY), pl.BlockSpec(memory_space=pltpu.VMEM)
    return pl.pallas_call(
        kernel,
        out_shape=[jax.ShapeDtypeStruct((2, 4, N, N), f32), jax.ShapeDtypeStruct(tile, f32)],
        in_specs=[hbm] * 3 + [pl.BlockSpec(memory_space=pltpu.SMEM)] * 3 + [local] * TABLES,
        out_specs=[local, local],
        scratch_shapes=[
            pltpu.VMEM((2, N, N), f32),
            pltpu.VMEM((2, 2, 64, ROWS, N), f32),
            pltpu.VMEM((2, 2, 64) + tile, f32),
            pltpu.VMEM((2, 2, 64, HALF), f32),
            pltpu.VMEM((2, 2, 64, HALF), f32),
            pltpu.VMEM((64, 2) + tile, f32),
            pltpu.VMEM((64, 2) + tile, f32),
            pltpu.VMEM((5, 12, 2) + tile, f32),
            pltpu.VMEM((GX * SENT, HALF), f32),
            pltpu.VMEM((GX * SENT, HALF), f32),
            pltpu.VMEM((GX * BACK, HALF), f32),
            pltpu.VMEM((GX * BACK, HALF), f32),
            pltpu.VMEM((64, 12) + tile, f32),
            pltpu.VMEM((GX, 4) + tile, f32),
            pltpu.VMEM((GX, 4) + tile, f32),
            pltpu.VMEM((GX, 4) + tile, f32),
            pltpu.VMEM((2, 10) + tile, f32),
            pltpu.VMEM((2, 3, 10) + tile, f32),
            pltpu.VMEM((GX,) + tile, f32),
            pltpu.VMEM((GX,) + tile, f32),
            pltpu.VMEM((ROWS, N), f32),
            dma((4,)),
            dma((len(OUTWARD),)),
            dma((len(HOMEWARD),)),
            dma((len(OUTWARD), GX)),
            dma((len(OUTWARD), GX)),
            dma((len(HOMEWARD), GX)),
            dma((len(HOMEWARD), GX)),
            dma((2, len(FLUXES), BA - 1)),
            dma((2, len(FLUXES), BA - 1)),
            dma((GX,)),
            dma((GX,)),
            dma((2,)),
            dma((2,)),
            dma((2,)),
            dma((2,)),
            dma((2, BA - 1)),
            dma((2, BA - 1)),
        ],
        compiler_params=pltpu.CompilerParams(collective_id=0, has_side_effects=True, vmem_limit_bytes=56 << 20),
        name="transport",
    )(phi, coeff, target, rates, speeds, shares, *tables())


def body(phi_start, coeff, forward, rates, speeds, shares):
    phi, sums = program(phi_start, coeff, forward, rates, speeds, shares)
    phi = phi * coeff[:, None]
    parts = sums[:, :24].reshape(2, 4, 2, 12)
    return (phi, jnp.transpose(parts[0] + parts[1], (1, 2, 0)))


def solution(mesh):
    in_specs = (
        P("gx", "ba", None, None),
        P("gx", None, None),
        P(None, None, None, "gx", None),
        P("ba"),
        P("ba"),
        P("ba"),
    )
    out_specs = (P("gx", "ba", None, None), P("gx", None, "ba"))
    return jax.shard_map(body, mesh=mesh, in_specs=in_specs, out_specs=out_specs, check_vma=False)
```

```python
import functools
import math

import jax
import jax.numpy as jnp
import numpy as np
from jax import lax
from jax.experimental import pallas as pl
from jax.experimental.pallas import tpu as pltpu
from jax.sharding import PartitionSpec as P

MESH = pl.DeviceIdType.MESH
N = 256
HALF = 128
GX = 32
BA = 4
ROWS = 8
BASE = 1.5 * 2.0 * math.pi / N


def quadrature():
    level = np.arange(6)
    polar = 0.2 + 0.15 * level
    cosine = np.concatenate([-polar, polar])
    azimuth = np.concatenate([level * (math.pi / 3.0) + math.pi / 6.0, level * (math.pi / 3.0)])
    sine = np.sqrt(1.0 - cosine * cosine)
    return cosine, sine * np.cos(azimuth), sine * np.sin(azimuth)


COS, SX, SY = quadrature()


def halves(table):
    table = jnp.asarray(table, jnp.float32)
    high = table.astype(jnp.bfloat16)
    return high, (table - high.astype(jnp.float32)).astype(jnp.bfloat16)


def np_halves(table):
    table = np.asarray(table, np.float32)
    high = table.astype(jnp.bfloat16)
    low = (table - high.astype(np.float32)).astype(jnp.bfloat16)
    return [jnp.asarray(high), jnp.asarray(low)]


def tables():
    index = np.arange(N)
    angle = (index[:, None] * index[None, :] % N) * (2.0 * np.pi / N)
    cos, sin = np.cos(angle) / 16.0, np.sin(angle) / 16.0
    rows = np.concatenate([cos[:, :HALF], -sin[:, :HALF]], axis=1)
    rows[:, HALF] = cos[:, HALF]
    back = np.concatenate([2.0 * cos[:HALF], -2.0 * sin[:HALF]], axis=0)
    back[0] = cos[0]
    back[HALF] = cos[HALF]
    order = np.arange(N).reshape(GX, ROWS).T.reshape(-1)
    stacks = [rows, back, cos, sin, cos[order], sin[order], cos[:, order], sin[:, order]]
    return [part for stack in stacks for part in np_halves(stack)]


def split(value):
    high = value.astype(jnp.bfloat16)
    return high, (value - high.astype(jnp.float32)).astype(jnp.bfloat16)


def product(left, right):
    lh, ll = left
    rh, rl = right
    dot = functools.partial(jnp.dot, preferred_element_type=jnp.float32)
    return dot(lh, rh) + (dot(ll, rh) + dot(lh, rl))


SENT = 136
BACK = 128
OUTWARD = ((0, 2), (2, 3), (5, 4), (9, 4), (13, 4))
HOMEWARD = ((0, 4), (4, 4), (8, 4), (12, 4))
FLUXES = ((0, 4), (4, 2), (6, 2), (8, 2))
TABLES = 16


def spot(t, zz, part):
    return 4 * t + 2 * zz + part + (1 if t > 0 else 0)


def tile_of(ref, row):
    return ref[pl.ds(pl.multiple_of(row, ROWS), ROWS), :]


def kernel(phi, coeff_in, target, rates, speeds, shares, *rest):
    names = [rest[2 * i : 2 * i + 2] for i in range(TABLES // 2)]
    wave_y, back_y, cos_x, sin_x, cos_rows, sin_rows, cos_cols, sin_cols = names
    (field, grads, coeff, held, mirror, lead, lead_in, goal, edge_goal, alpha, sent, spec, made, back, acc, espec,
     enew, epack, flux, others, gsum, gall, line_of, load, own, own_back, send, recv, send_back, recv_back, send_flux,
     recv_flux, send_grad, recv_grad, send_turn, recv_turn, send_lead, recv_lead, send_share, recv_share) = rest[TABLES:]
    gx, ba = lax.axis_index("gx"), lax.axis_index("ba")
    barrier = pltpu.get_barrier_semaphore()

    def greet(k, carry):
        pl.semaphore_signal(barrier, inc=1, device_id=(lax.rem(gx + k, GX), ba), device_id_type=MESH)
        return carry

    lax.fori_loop(1, GX, greet, 0)
    for k in range(1, BA):
        pl.semaphore_signal(barrier, inc=1, device_id=(gx, lax.rem(ba + k, BA)), device_id_type=MESH)

    loads = [
        pltpu.make_async_copy(phi.at[0], field.at[0], load.at[0]),
        pltpu.make_async_copy(phi.at[1], field.at[1], load.at[1]),
        pltpu.make_async_copy(target, held, load.at[2]),
        pltpu.make_async_copy(coeff_in, coeff, load.at[3]),
    ]
    for copy in loads:
        copy.start()

    sub = lax.broadcasted_iota(jnp.int32, (ROWS, HALF), 0)
    lane = lax.broadcasted_iota(jnp.int32, (ROWS, HALF), 1)
    upper = sub < 4

    def by_band(values):
        spread = jnp.where(sub % 4 == 0, values[0], values[1])
        return jnp.where(sub % 4 >= 2, jnp.where(sub % 4 == 2, values[2], values[3]), spread)

    rate, speed, share = by_band(rates), by_band(speeds), by_band(shares)
    couple = [speed * float(abs(COS[d])) for d in range(6)]
    zero = jnp.zeros((ROWS, HALF), jnp.float32)

    def clear(z, carry):
        for d in range(12):
            acc[z, d] = zero
        return carry

    lax.fori_loop(0, 64, clear, 0)

    def signed(index):
        return (lax.rem(index + HALF, N) - HALF).astype(jnp.float32) * BASE

    def propagators():
        for t in range(5):
            if t < 4:
                fx, fy = signed(gx * ROWS + 2 * t + sub // 4), signed(lane)
            else:
                kx = gx * ROWS + lane % ROWS
                line = signed(kx)
                line = jnp.where((lane >= 8) & (kx == HALF), -line, line)
                fx = jnp.where(upper, line, HALF * BASE)
                fy = jnp.where(upper, jnp.where(lane < 8, -HALF * BASE, HALF * BASE), signed(lane))
            for d in range(12):
                wave = speed * (fx * float(SX[d]) + fy * float(SY[d]))
                real = rate + speed * float(abs(COS[d]))
                denom = real * real + wave * wave
                alpha[t, d, 0] = real / denom
                alpha[t, d, 1] = -wave / denom

    partner, first_row = GX - 1 - gx, lax.rem(GX - gx, GX)
    quarter = pl.ds(pl.multiple_of(ba * 16, 16), 16)

    def turn_copy(s):
        return pltpu.make_async_remote_copy(
            src_ref=held.at[s, :, quarter, :, pl.ds(HALF, HALF)],
            dst_ref=mirror.at[s, :, quarter],
            send_sem=send_turn.at[s],
            recv_sem=recv_turn.at[s],
            device_id=(partner, ba),
            device_id_type=MESH,
        )

    def share_copy(s, k):
        return pltpu.make_async_remote_copy(
            src_ref=mirror.at[s, :, quarter],
            dst_ref=mirror.at[s, :, quarter],
            send_sem=send_share.at[s, k - 1],
            recv_sem=recv_share.at[s, k - 1],
            device_id=(gx, lax.rem(ba + k, BA)),
            device_id_type=MESH,
        )

    def lead_copy(s):
        return pltpu.make_async_remote_copy(
            src_ref=lead.at[s],
            dst_ref=lead_in.at[s],
            send_sem=send_lead.at[s],
            recv_sem=recv_lead.at[s],
            device_id=(first_row, ba),
            device_id_type=MESH,
        )

    def lead_rows(s):
        for c in range(2):
            lead[s, c] = held[s, c, :, 0, HALF:]

    def start_turn(s):
        turn_copy(s).start()

        @pl.when(first_row != gx)
        def _():
            lead_copy(s).start()

    def start_share(s):
        turn_copy(s).wait_recv()
        for k in range(1, BA):
            share_copy(s, k).start()

    def fold(s):
        for k in range(1, BA):
            share_copy(s, k).wait_recv()

        @pl.when(first_row != gx)
        def _():
            lead_copy(s).wait_recv()

        @pl.when(first_row == gx)
        def _():
            lead_in[s] = lead[s]

        lanes = lax.rem(HALF - lane, HALF)
        rows = lax.rem(ROWS - sub, ROWS)
        keep = (lane > 0) & ((gx != HALF // ROWS) | (sub > 0))
        alone = (lane > 0) & (gx == HALF // ROWS)

        def cell(block, carry):
            for z, c in [(8 * block + i, c) for i in range(8) for c in range(2)]:
                tile = jnp.where(sub == 0, lead_in[s, c, pl.ds(z, 1), :], mirror[s, c, z])
                tile = jnp.take_along_axis(jnp.take_along_axis(tile, lanes, axis=1), rows, axis=0)
                tile = jnp.where(keep, tile, 0.0)
                low, high = held[s, c, z, :, :HALF], held[s, c, z, :, HALF:]
                goal[z, c] = low + tile if c == 0 else low - tile
                line = jnp.sum(jnp.where(lane == sub, jnp.broadcast_to(high[:, 0:1], (ROWS, HALF)), 0.0), axis=0, keepdims=True)
                other = jnp.where(alone, jnp.take_along_axis(high, lanes, axis=1), 0.0)
                other = other[0:1] if c == 0 else -other[0:1]
                edge_goal[z, c] = jnp.where(upper, line, other)
            return carry

        lax.fori_loop(0, 8, cell, 0)

    def turns_done():
        for s in range(2):
            turn_copy(s).wait_send()
            for k in range(1, BA):
                share_copy(s, k).wait_send()

            @pl.when(first_row != gx)
            def _():
                lead_copy(s).wait_send()

    def outward(message, k):
        first, count = OUTWARD[message]
        to = lax.rem(gx + k, GX)
        return pltpu.make_async_remote_copy(
            src_ref=sent.at[pl.ds(pl.multiple_of(to * SENT + first * ROWS, ROWS), count * ROWS), :],
            dst_ref=spec.at[pl.ds(pl.multiple_of(gx * SENT + first * ROWS, ROWS), count * ROWS), :],
            send_sem=send.at[message, k],
            recv_sem=recv.at[message, k],
            device_id=(to, ba),
            device_id_type=MESH,
        )

    def outward_own(message):
        first, count = OUTWARD[message]
        rows = pl.ds(pl.multiple_of(gx * SENT + first * ROWS, ROWS), count * ROWS)
        return pltpu.make_async_copy(sent.at[rows, :], spec.at[rows, :], own.at[message])

    def homeward(message, k):
        first, count = HOMEWARD[message]
        to = lax.rem(gx + k, GX)
        return pltpu.make_async_remote_copy(
            src_ref=made.at[pl.ds(pl.multiple_of(to * BACK + first * ROWS, ROWS), count * ROWS), :],
            dst_ref=back.at[pl.ds(pl.multiple_of(gx * BACK + first * ROWS, ROWS), count * ROWS), :],
            send_sem=send_back.at[message, k],
            recv_sem=recv_back.at[message, k],
            device_id=(to, ba),
            device_id_type=MESH,
        )

    def homeward_own(message):
        first, count = HOMEWARD[message]
        rows = pl.ds(pl.multiple_of(gx * BACK + first * ROWS, ROWS), count * ROWS)
        return pltpu.make_async_copy(made.at[rows, :], back.at[rows, :], own_back.at[message])

    def wall_copy(s, message, k):
        first, count = FLUXES[message]
        return pltpu.make_async_remote_copy(
            src_ref=flux.at[s, pl.ds(first, count)],
            dst_ref=others.at[s, k - 1, pl.ds(first, count)],
            send_sem=send_flux.at[s, message, k - 1],
            recv_sem=recv_flux.at[s, message, k - 1],
            device_id=(gx, lax.rem(ba + k, BA)),
            device_id_type=MESH,
        )

    def grad_copy(k):
        to = lax.rem(gx + k, GX)
        return pltpu.make_async_remote_copy(
            src_ref=gsum.at[to],
            dst_ref=gall.at[gx],
            send_sem=send_grad.at[k],
            recv_sem=recv_grad.at[k],
            device_id=(to, ba),
            device_id_type=MESH,
        )

    def over_peers(act):
        def one(k, carry):
            act(k)
            return carry

        lax.fori_loop(1, GX, one, 0)

    def start_outward(message):
        outward_own(message).start()
        over_peers(lambda k: outward(message, k).start())

    def wait_outward(message):
        outward_own(message).wait()
        over_peers(lambda k: outward(message, k).wait_recv())

    def start_homeward(message):
        homeward_own(message).start()
        over_peers(lambda k: homeward(message, k).start())

    def wait_homeward():
        for message in range(len(HOMEWARD)):
            homeward_own(message).wait()
            over_peers(lambda k: homeward(message, k).wait_recv())

    def sends_done(s):
        for message in range(len(OUTWARD)):
            over_peers(lambda k: outward(message, k).wait_send())
        for message in range(len(HOMEWARD)):
            over_peers(lambda k: homeward(message, k).wait_send())
        for message in range(len(FLUXES)):
            for k in range(1, BA):
                wall_copy(s, message, k).wait_send()

    inner = lax.broadcasted_iota(jnp.int32, (N, HALF), 1) != 0
    row8 = lax.broadcasted_iota(jnp.int32, (ROWS, N), 0)
    sign = jnp.where(lax.broadcasted_iota(jnp.int32, (ROWS, N), 1) % 2 == 0, 1.0 / 16.0, -1.0 / 16.0)

    def both(pair):
        return pair[0][...], pair[1][...]

    def forward(zz):
        def plane(b, carry):
            value = split(field[zz, b])
            rows = split(product(value, both(wave_y)))
            u = product(both(cos_rows), rows)
            v = product(both(sin_rows), rows)
            re = u[:, :HALF] + jnp.where(inner, v[:, HALF:], 0.0)
            im = jnp.where(inner, u[:, HALF:], 0.0) - v[:, :HALF]
            for t in range(4):
                for r in range(2):
                    for m in range(0, GX, ROWS):
                        at = (2 * t + r) * GX + m
                        for part, value_ in ((0, re), (1, im)):
                            row = m * SENT + spot(t, zz, part) * ROWS + r * 4
                            sent[pl.ds(row + b, ROWS, stride=SENT), :] = value_[at : at + ROWS]
            pick = jnp.where(row8 == zz * 4 + b, sign, 0.0).astype(jnp.bfloat16)
            nt = (((1,), (1,)), ((), ()))
            line_of[...] += lax.dot_general(
                pick, value[0], nt, preferred_element_type=jnp.float32
            ) + lax.dot_general(pick, value[1], nt, preferred_element_type=jnp.float32)
            return carry

        lax.fori_loop(0, 4, plane, 0)

    def edges():
        line = split(line_of[...])
        line_re = product(line, both(cos_x))
        line_im = -product(line, both(sin_x))
        for m in range(GX):
            at, off = HALF * (m // 16), 8 * (m % 16)
            re, im = line_re[:, at : at + HALF], line_im[:, at : at + HALF]
            tile = jnp.where(lane < 8, pltpu.roll(re, (HALF - off) % HALF, 1), 0.0)
            tile = jnp.where((lane >= 8) & (lane < 16), pltpu.roll(re, (HALF + 8 - off) % HALF, 1), tile)
            tile = jnp.where((lane >= 64) & (lane < 72), pltpu.roll(im, (HALF + 64 - off) % HALF, 1), tile)
            tile = jnp.where((lane >= 72) & (lane < 80), pltpu.roll(im, (HALF + 72 - off) % HALF, 1), tile)
            sent[m * SENT + 32 : m * SENT + 40, :] = tile

    def inverse(zz, last):
        def plane(b, carry):
            parts = []
            for part in range(2):
                pieces = []
                for t in range(4):
                    for r in range(2):
                        for m in range(0, GX, ROWS):
                            row = m * BACK + (4 * t + 2 * zz + part) * ROWS + r * 4
                            pieces.append(back[pl.ds(row + b, ROWS, stride=BACK), :])
                parts.append(jnp.concatenate(pieces, axis=0))
            modes = split(jnp.concatenate(parts, axis=1))
            u = product(both(cos_cols), modes)
            v = product(both(sin_cols), modes)
            rows = jnp.concatenate([u[:, :HALF] - v[:, HALF:], u[:, HALF:] + v[:, :HALF]], axis=1)
            value = product(split(rows), both(back_y))
            field[zz, b] = value if last else value * coeff[zz]
            return carry

        lax.fori_loop(0, 4, plane, 0)

    def gather():
        def one(block, carry):
            for src, zz in [(4 * block + i, zz) for i in range(4) for zz in range(2)]:
                base = src * SENT
                line = tile_of(spec, base + 4 * ROWS)
                col = line if zz == 0 else pltpu.roll(line, 4, 0)
                col_re = jnp.where(lane < 16, col, 0.0)
                col_im = jnp.where(lane < 16, pltpu.roll(col, 64, 1), 0.0)
                espec[src, zz] = jnp.where(upper, col_re, pltpu.roll(tile_of(spec, base + spot(0, zz, 0) * ROWS), 4, 0))
                espec[src, 2 + zz] = jnp.where(
                    upper, col_im, pltpu.roll(tile_of(spec, base + spot(0, zz, 1) * ROWS), 4, 0)
                )
            return carry

        lax.fori_loop(0, GX // 4, one, 0)

    mean = jnp.where(upper & (gx == HALF // ROWS), 0.5, 0.0)

    def sweep(s, t, first, start_re, start_im):
        edge = t == 4
        inv = [(alpha[t, first + d, 0], alpha[t, first + d, 1]) for d in range(6)]

        def cells(step, psi):
            src = (GX - 1 - step) if first == 0 else step
            psi = list(psi)
            for zz in (1, 0) if first == 0 else (0, 1):
                z = 2 * src + zz
                if edge:
                    s_re, s_im = espec[src, zz], espec[src, 2 + zz]
                    g = [edge_goal[z, c] for c in range(2)]
                else:
                    s_re = tile_of(spec, src * SENT + spot(t, zz, 0) * ROWS)
                    s_im = tile_of(spec, src * SENT + spot(t, zz, 1) * ROWS)
                    g = [
                        jnp.where(upper, goal[z, c, 2 * t : 2 * t + 1], goal[z, c, 2 * t + 1 : 2 * t + 2])
                        for c in range(2)
                    ]
                s_re, s_im = s_re * rate, s_im * rate
                sums = [None, None]
                for d in range(6):
                    t_re = s_re + couple[d] * psi[2 * d]
                    t_im = s_im + couple[d] * psi[2 * d + 1]
                    p_re = inv[d][0] * t_re - inv[d][1] * t_im
                    p_im = inv[d][0] * t_im + inv[d][1] * t_re
                    psi[2 * d], psi[2 * d + 1] = p_re, p_im
                    sums = [p_re, p_im] if d == 0 else [sums[0] + p_re, sums[1] + p_im]
                    acc[z, first + d] += p_re * g[0] + p_im * g[1]
                if edge:
                    if first == 0:
                        enew[src, zz], enew[src, 2 + zz] = sums
                        continue
                    for c in range(2):
                        e = (enew[src, 2 * c + zz] + sums[c]) * (1.0 / 12.0)
                        enew[src, 2 * c + zz] = pltpu.roll(e, 4, 0)
                        h = 0.5 * (e + pltpu.roll(e, HALF - 8, 1))
                        epack[src, 2 * c + zz] = jnp.where(
                            upper, h, pltpu.roll(pltpu.roll(h, 4, 0), HALF - 1, 1)
                        )
                    continue
                for c in range(2):
                    rows = pl.ds(pl.multiple_of(src * BACK + (4 * t + 2 * zz + c) * ROWS, ROWS), ROWS)
                    if first == 0:
                        made[rows, :] = sums[c]
                        continue
                    total = (made[rows, :] + sums[c]) * (1.0 / 12.0)
                    if t == 0:
                        total = total + mean * (enew[src, 2 * c + zz] - total)
                    x = epack[src, 2 * (1 - c) + zz]
                    x = jnp.where(lane == 0, x if t == 0 else pltpu.roll(x, HALF - 2 * t, 1), 0.0)
                    made[rows, :] = total - x if c == 0 else total + x
            return tuple(psi)

        return lax.fori_loop(0, GX, cells, tuple([start_re, start_im] * 6))

    def down(s, t):
        psi = sweep(s, t, 0, zero, zero)
        at = 0 if t == 4 else 2 * t + 2
        for c in range(2):
            total = psi[c] * float(abs(COS[0]) / 12.0)
            for d in range(1, 6):
                total = total + psi[2 * d + c] * float(abs(COS[d]) / 12.0)
            flux[s, at + c] = total

    odd, second = sub % 2 == 1, sub % 4 >= 2

    def up(s, t):
        at = 0 if t == 4 else 2 * t + 2
        starts = []
        for c in range(2):
            total = flux[s, at + c] + others[s, 0, at + c] + others[s, 1, at + c] + others[s, 2, at + c]
            total = total + jnp.where(odd, pltpu.roll(total, 1, 0), pltpu.roll(total, ROWS - 1, 0))
            total = total + jnp.where(second, pltpu.roll(total, 2, 0), pltpu.roll(total, ROWS - 2, 0))
            starts.append(total * share)
        sweep(s, t, 6, *starts)

    def start_wall(s, message):
        for k in range(1, BA):
            wall_copy(s, message, k).start()

    def wait_wall(s, message):
        for k in range(1, BA):
            wall_copy(s, message, k).wait_recv()

    propagators()
    loads[2].wait()
    for s in range(2):
        lead_rows(s)
    pl.semaphore_wait(barrier, GX - 1 + BA - 1)
    for s in range(2):
        start_turn(s)

    def one_step(s, carry):
        line_of[...] = jnp.zeros_like(line_of)

        @pl.when(s > 0)
        def _():
            wait_homeward()
            sends_done(s - 1)
            inverse(0, False)

        @pl.when(s == 0)
        def _():
            loads[0].wait()

        forward(0)
        start_outward(0)

        @pl.when(s > 0)
        def _():
            inverse(1, False)

        @pl.when(s == 0)
        def _():
            for copy in (loads[1], loads[3]):
                copy.wait()

        forward(1)
        edges()

        @pl.when(s == 0)
        def _():
            start_share(0)
            start_share(1)

        start_outward(1)
        start_outward(2)
        fold(s)
        wait_outward(0)
        wait_outward(1)
        gather()
        down(s, 4)
        down(s, 0)
        start_wall(s, 0)
        start_outward(3)
        wait_outward(2)
        down(s, 1)
        start_wall(s, 1)
        start_outward(4)
        wait_wall(s, 0)
        up(s, 4)
        up(s, 0)
        start_homeward(0)
        for t in (1, 2):
            wait_outward(t + 2)
            down(s, t + 1)
            start_wall(s, t + 1)
            wait_wall(s, t)
            up(s, t)
            start_homeward(t)
        wait_wall(s, 3)
        up(s, 3)
        start_homeward(3)
        return carry

    lax.fori_loop(0, 2, one_step, 0)

    def reduce(src, carry):
        tile = zero
        for zz in range(2):
            for d in range(12):
                total = jnp.sum(acc[2 * src + zz, d], axis=1, keepdims=True)
                tile = jnp.where(lane == zz * 12 + d, total, tile)
        gsum[src] = tile * (1.0 / N)
        return carry

    lax.fori_loop(0, GX, reduce, 0)
    over_peers(lambda k: grad_copy(k).start())
    wait_homeward()
    for zz in range(2):
        inverse(zz, True)
    over_peers(lambda k: grad_copy(k).wait())
    gall[gx] = gsum[gx]
    total = gall[0]
    for src in range(1, GX):
        total = total + gall[src]
    grads[...] = total
    sends_done(1)
    turns_done()


def program(phi, coeff, target, rates, speeds, shares):
    f32 = jnp.float32
    dma = pltpu.SemaphoreType.DMA
    tile = (ROWS, HALF)
    hbm, local = pl.BlockSpec(memory_space=pl.ANY), pl.BlockSpec(memory_space=pltpu.VMEM)
    return pl.pallas_call(
        kernel,
        out_shape=[jax.ShapeDtypeStruct((2, 4, N, N), f32), jax.ShapeDtypeStruct(tile, f32)],
        in_specs=[hbm] * 3 + [pl.BlockSpec(memory_space=pltpu.SMEM)] * 3 + [local] * TABLES,
        out_specs=[local, local],
        scratch_shapes=[
            pltpu.VMEM((2, N, N), f32),
            pltpu.VMEM((2, 2, 64, ROWS, N), f32),
            pltpu.VMEM((2, 2, 64) + tile, f32),
            pltpu.VMEM((2, 2, 64, HALF), f32),
            pltpu.VMEM((2, 2, 64, HALF), f32),
            pltpu.VMEM((64, 2) + tile, f32),
            pltpu.VMEM((64, 2) + tile, f32),
            pltpu.VMEM((5, 12, 2) + tile, f32),
            pltpu.VMEM((GX * SENT, HALF), f32),
            pltpu.VMEM((GX * SENT, HALF), f32),
            pltpu.VMEM((GX * BACK, HALF), f32),
            pltpu.VMEM((GX * BACK, HALF), f32),
            pltpu.VMEM((64, 12) + tile, f32),
            pltpu.VMEM((GX, 4) + tile, f32),
            pltpu.VMEM((GX, 4) + tile, f32),
            pltpu.VMEM((GX, 4) + tile, f32),
            pltpu.VMEM((2, 10) + tile, f32),
            pltpu.VMEM((2, 3, 10) + tile, f32),
            pltpu.VMEM((GX,) + tile, f32),
            pltpu.VMEM((GX,) + tile, f32),
            pltpu.VMEM((ROWS, N), f32),
            dma((4,)),
            dma((len(OUTWARD),)),
            dma((len(HOMEWARD),)),
            dma((len(OUTWARD), GX)),
            dma((len(OUTWARD), GX)),
            dma((len(HOMEWARD), GX)),
            dma((len(HOMEWARD), GX)),
            dma((2, len(FLUXES), BA - 1)),
            dma((2, len(FLUXES), BA - 1)),
            dma((GX,)),
            dma((GX,)),
            dma((2,)),
            dma((2,)),
            dma((2,)),
            dma((2,)),
            dma((2, BA - 1)),
            dma((2, BA - 1)),
        ],
        compiler_params=pltpu.CompilerParams(collective_id=0, has_side_effects=True, vmem_limit_bytes=56 << 20),
        name="transport",
    )(phi, coeff, target, rates, speeds, shares, *tables())


def body(phi_start, coeff, forward, rates, speeds, shares):
    phi, sums = program(phi_start, coeff, forward, rates, speeds, shares)
    phi = phi * coeff[:, None]
    parts = sums[:, :24].reshape(2, 4, 2, 12)
    return (phi, jnp.transpose(parts[0] + parts[1], (1, 2, 0)))


def solution(mesh):
    in_specs = (
        P("gx", "ba", None, None),
        P("gx", None, None),
        P(None, None, None, "gx", None),
        P("ba"),
        P("ba"),
        P("ba"),
    )
    out_specs = (P("gx", "ba", None, None), P("gx", None, "ba"))
    return jax.shard_map(body, mesh=mesh, in_specs=in_specs, out_specs=out_specs, check_vma=False)
```

```python
import functools
import math

import jax
import jax.numpy as jnp
import numpy as np
from jax import lax
from jax.experimental import pallas as pl
from jax.experimental.pallas import tpu as pltpu
from jax.sharding import PartitionSpec as P

MESH = pl.DeviceIdType.MESH
N = 256
HALF = 128
GX = 32
BA = 4
ROWS = 8
BASE = 1.5 * 2.0 * math.pi / N


def quadrature():
    level = np.arange(6)
    polar = 0.2 + 0.15 * level
    cosine = np.concatenate([-polar, polar])
    azimuth = np.concatenate([level * (math.pi / 3.0) + math.pi / 6.0, level * (math.pi / 3.0)])
    sine = np.sqrt(1.0 - cosine * cosine)
    return cosine, sine * np.cos(azimuth), sine * np.sin(azimuth)


COS, SX, SY = quadrature()


def halves(table):
    table = jnp.asarray(table, jnp.float32)
    high = table.astype(jnp.bfloat16)
    return high, (table - high.astype(jnp.float32)).astype(jnp.bfloat16)


def np_halves(table):
    table = np.asarray(table, np.float32)
    high = table.astype(jnp.bfloat16)
    low = (table - high.astype(np.float32)).astype(jnp.bfloat16)
    return [jnp.asarray(high), jnp.asarray(low)]


def tables():
    index = np.arange(N)
    angle = (index[:, None] * index[None, :] % N) * (2.0 * np.pi / N)
    cos, sin = np.cos(angle) / 16.0, np.sin(angle) / 16.0
    rows = np.concatenate([cos[:, :HALF], -sin[:, :HALF]], axis=1)
    rows[:, HALF] = cos[:, HALF]
    back = np.concatenate([2.0 * cos[:HALF], -2.0 * sin[:HALF]], axis=0)
    back[0] = cos[0]
    back[HALF] = cos[HALF]
    order = np.arange(N).reshape(GX, ROWS).T.reshape(-1)
    stacks = [rows, back, cos, sin, cos[order], sin[order], cos[:, order], sin[:, order]]
    return [part for stack in stacks for part in np_halves(stack)]


def split(value):
    high = value.astype(jnp.bfloat16)
    return high, (value - high.astype(jnp.float32)).astype(jnp.bfloat16)


def product(left, right):
    lh, ll = left
    rh, rl = right
    dot = functools.partial(jnp.dot, preferred_element_type=jnp.float32)
    return dot(lh, rh) + (dot(ll, rh) + dot(lh, rl))


SENT = 136
BACK = 128
OUTWARD = ((0, 2), (2, 3), (5, 4), (9, 4), (13, 4))
HOMEWARD = ((0, 4), (4, 4), (8, 4), (12, 4))
FLUXES = ((0, 4), (4, 2), (6, 2), (8, 2))
TABLES = 16


def spot(t, zz, part):
    return 4 * t + 2 * zz + part + (1 if t > 0 else 0)


def tile_of(ref, row):
    return ref[pl.ds(pl.multiple_of(row, ROWS), ROWS), :]


def kernel(phi, coeff_in, target, rates, speeds, shares, *rest):
    names = [rest[2 * i : 2 * i + 2] for i in range(TABLES // 2)]
    wave_y, back_y, cos_x, sin_x, cos_rows, sin_rows, cos_cols, sin_cols = names
    (field, grads, coeff, held, mirror, lead, lead_in, goal, edge_goal, alpha, sent, spec, made, back, acc, espec,
     enew, epack, flux, others, gsum, gall, line_of, load, own, own_back, send, recv, send_back, recv_back, send_flux,
     recv_flux, send_grad, recv_grad, send_turn, recv_turn, send_lead, recv_lead, send_share, recv_share) = rest[TABLES:]
    gx, ba = lax.axis_index("gx"), lax.axis_index("ba")
    barrier = pltpu.get_barrier_semaphore()

    def greet(k, carry):
        pl.semaphore_signal(barrier, inc=1, device_id=(lax.rem(gx + k, GX), ba), device_id_type=MESH)
        return carry

    lax.fori_loop(1, GX, greet, 0)
    for k in range(1, BA):
        pl.semaphore_signal(barrier, inc=1, device_id=(gx, lax.rem(ba + k, BA)), device_id_type=MESH)

    loads = [
        pltpu.make_async_copy(phi.at[0], field.at[0], load.at[0]),
        pltpu.make_async_copy(phi.at[1], field.at[1], load.at[1]),
        pltpu.make_async_copy(target, held, load.at[2]),
        pltpu.make_async_copy(coeff_in, coeff, load.at[3]),
    ]
    for copy in loads:
        copy.start()

    sub = lax.broadcasted_iota(jnp.int32, (ROWS, HALF), 0)
    lane = lax.broadcasted_iota(jnp.int32, (ROWS, HALF), 1)
    upper = sub < 4

    def by_band(values):
        spread = jnp.where(sub % 4 == 0, values[0], values[1])
        return jnp.where(sub % 4 >= 2, jnp.where(sub % 4 == 2, values[2], values[3]), spread)

    rate, speed, share = by_band(rates), by_band(speeds), by_band(shares)
    couple = [speed * float(abs(COS[d])) for d in range(6)]
    zero = jnp.zeros((ROWS, HALF), jnp.float32)

    def clear(z, carry):
        for d in range(12):
            acc[z, d] = zero
        return carry

    lax.fori_loop(0, 64, clear, 0)

    def signed(index):
        return (lax.rem(index + HALF, N) - HALF).astype(jnp.float32) * BASE

    def propagators():
        for t in range(5):
            if t < 4:
                fx, fy = signed(gx * ROWS + 2 * t + sub // 4), signed(lane)
            else:
                kx = gx * ROWS + lane % ROWS
                line = signed(kx)
                line = jnp.where((lane >= 8) & (kx == HALF), -line, line)
                fx = jnp.where(upper, line, HALF * BASE)
                fy = jnp.where(upper, jnp.where(lane < 8, -HALF * BASE, HALF * BASE), signed(lane))
            for d in range(12):
                wave = speed * (fx * float(SX[d]) + fy * float(SY[d]))
                real = rate + speed * float(abs(COS[d]))
                denom = real * real + wave * wave
                alpha[t, d, 0] = real / denom
                alpha[t, d, 1] = -wave / denom

    partner, first_row = GX - 1 - gx, lax.rem(GX - gx, GX)
    quarter = pl.ds(pl.multiple_of(ba * 16, 16), 16)

    def turn_copy(s):
        return pltpu.make_async_remote_copy(
            src_ref=held.at[s, :, quarter, :, pl.ds(HALF, HALF)],
            dst_ref=mirror.at[s, :, quarter],
            send_sem=send_turn.at[s],
            recv_sem=recv_turn.at[s],
            device_id=(partner, ba),
            device_id_type=MESH,
        )

    def share_copy(s, k):
        return pltpu.make_async_remote_copy(
            src_ref=mirror.at[s, :, quarter],
            dst_ref=mirror.at[s, :, quarter],
            send_sem=send_share.at[s, k - 1],
            recv_sem=recv_share.at[s, k - 1],
            device_id=(gx, lax.rem(ba + k, BA)),
            device_id_type=MESH,
        )

    def lead_copy(s):
        return pltpu.make_async_remote_copy(
            src_ref=lead.at[s],
            dst_ref=lead_in.at[s],
            send_sem=send_lead.at[s],
            recv_sem=recv_lead.at[s],
            device_id=(first_row, ba),
            device_id_type=MESH,
        )

    def lead_rows(s):
        for c in range(2):
            lead[s, c] = held[s, c, :, 0, HALF:]

    def start_turn(s):
        turn_copy(s).start()

        @pl.when(first_row != gx)
        def _():
            lead_copy(s).start()

    def start_share(s):
        turn_copy(s).wait_recv()
        for k in range(1, BA):
            share_copy(s, k).start()

    def fold(s):
        for k in range(1, BA):
            share_copy(s, k).wait_recv()

        @pl.when(first_row != gx)
        def _():
            lead_copy(s).wait_recv()

        @pl.when(first_row == gx)
        def _():
            lead_in[s] = lead[s]

        lanes = lax.rem(HALF - lane, HALF)
        rows = lax.rem(ROWS - sub, ROWS)
        keep = (lane > 0) & ((gx != HALF // ROWS) | (sub > 0))
        alone = (lane > 0) & (gx == HALF // ROWS)

        def cell(block, carry):
            for z, c in [(8 * block + i, c) for i in range(8) for c in range(2)]:
                tile = jnp.where(sub == 0, lead_in[s, c, pl.ds(z, 1), :], mirror[s, c, z])
                tile = jnp.take_along_axis(jnp.take_along_axis(tile, lanes, axis=1), rows, axis=0)
                tile = jnp.where(keep, tile, 0.0)
                low, high = held[s, c, z, :, :HALF], held[s, c, z, :, HALF:]
                goal[z, c] = low + tile if c == 0 else low - tile
                line = jnp.sum(jnp.where(lane == sub, jnp.broadcast_to(high[:, 0:1], (ROWS, HALF)), 0.0), axis=0, keepdims=True)
                other = jnp.where(alone, jnp.take_along_axis(high, lanes, axis=1), 0.0)
                other = other[0:1] if c == 0 else -other[0:1]
                edge_goal[z, c] = jnp.where(upper, line, other)
            return carry

        lax.fori_loop(0, 8, cell, 0)

    def turns_done():
        for s in range(2):
            turn_copy(s).wait_send()
            for k in range(1, BA):
                share_copy(s, k).wait_send()

            @pl.when(first_row != gx)
            def _():
                lead_copy(s).wait_send()

    def outward(message, k):
        first, count = OUTWARD[message]
        to = lax.rem(gx + k, GX)
        return pltpu.make_async_remote_copy(
            src_ref=sent.at[pl.ds(pl.multiple_of(to * SENT + first * ROWS, ROWS), count * ROWS), :],
            dst_ref=spec.at[pl.ds(pl.multiple_of(gx * SENT + first * ROWS, ROWS), count * ROWS), :],
            send_sem=send.at[message, k],
            recv_sem=recv.at[message, k],
            device_id=(to, ba),
            device_id_type=MESH,
        )

    def outward_own(message):
        first, count = OUTWARD[message]
        rows = pl.ds(pl.multiple_of(gx * SENT + first * ROWS, ROWS), count * ROWS)
        return pltpu.make_async_copy(sent.at[rows, :], spec.at[rows, :], own.at[message])

    def homeward(message, k):
        first, count = HOMEWARD[message]
        to = lax.rem(gx + k, GX)
        return pltpu.make_async_remote_copy(
            src_ref=made.at[pl.ds(pl.multiple_of(to * BACK + first * ROWS, ROWS), count * ROWS), :],
            dst_ref=back.at[pl.ds(pl.multiple_of(gx * BACK + first * ROWS, ROWS), count * ROWS), :],
            send_sem=send_back.at[message, k],
            recv_sem=recv_back.at[message, k],
            device_id=(to, ba),
            device_id_type=MESH,
        )

    def homeward_own(message):
        first, count = HOMEWARD[message]
        rows = pl.ds(pl.multiple_of(gx * BACK + first * ROWS, ROWS), count * ROWS)
        return pltpu.make_async_copy(made.at[rows, :], back.at[rows, :], own_back.at[message])

    def wall_copy(s, message, k):
        first, count = FLUXES[message]
        return pltpu.make_async_remote_copy(
            src_ref=flux.at[s, pl.ds(first, count)],
            dst_ref=others.at[s, k - 1, pl.ds(first, count)],
            send_sem=send_flux.at[s, message, k - 1],
            recv_sem=recv_flux.at[s, message, k - 1],
            device_id=(gx, lax.rem(ba + k, BA)),
            device_id_type=MESH,
        )

    def grad_copy(k):
        to = lax.rem(gx + k, GX)
        return pltpu.make_async_remote_copy(
            src_ref=gsum.at[to],
            dst_ref=gall.at[gx],
            send_sem=send_grad.at[k],
            recv_sem=recv_grad.at[k],
            device_id=(to, ba),
            device_id_type=MESH,
        )

    def over_peers(act):
        def one(k, carry):
            act(k)
            return carry

        lax.fori_loop(1, GX, one, 0)

    def start_outward(message):
        outward_own(message).start()
        over_peers(lambda k: outward(message, k).start())

    def wait_outward(message):
        outward_own(message).wait()
        over_peers(lambda k: outward(message, k).wait_recv())

    def start_homeward(message):
        homeward_own(message).start()
        over_peers(lambda k: homeward(message, k).start())

    def wait_homeward():
        for message in range(len(HOMEWARD)):
            homeward_own(message).wait()
            over_peers(lambda k: homeward(message, k).wait_recv())

    def sends_done(s):
        for message in range(len(OUTWARD)):
            over_peers(lambda k: outward(message, k).wait_send())
        for message in range(len(HOMEWARD)):
            over_peers(lambda k: homeward(message, k).wait_send())
        for message in range(len(FLUXES)):
            for k in range(1, BA):
                wall_copy(s, message, k).wait_send()

    inner = lax.broadcasted_iota(jnp.int32, (N, HALF), 1) != 0
    row8 = lax.broadcasted_iota(jnp.int32, (ROWS, N), 0)
    sign = jnp.where(lax.broadcasted_iota(jnp.int32, (ROWS, N), 1) % 2 == 0, 1.0 / 16.0, -1.0 / 16.0)

    def both(pair):
        return pair[0][...], pair[1][...]

    def forward(zz):
        def planes(pair, carry):
            both_b = (2 * pair, 2 * pair + 1)
            values = [split(field[zz, b]) for b in both_b]
            rows = [split(product(value, both(wave_y))) for value in values]
            us = [product(both(cos_rows), row) for row in rows]
            vs = [product(both(sin_rows), row) for row in rows]
            for b, u, v in zip(both_b, us, vs):
                re = u[:, :HALF] + jnp.where(inner, v[:, HALF:], 0.0)
                im = jnp.where(inner, u[:, HALF:], 0.0) - v[:, :HALF]
                for t in range(4):
                    for r in range(2):
                        for m in range(0, GX, ROWS):
                            at = (2 * t + r) * GX + m
                            for part, value in ((0, re), (1, im)):
                                row = m * SENT + spot(t, zz, part) * ROWS + r * 4
                                sent[pl.ds(row + b, ROWS, stride=SENT), :] = value[at : at + ROWS]
            nt = (((1,), (1,)), ((), ()))
            total = line_of[...]
            for b, value in zip(both_b, values):
                pick = jnp.where(row8 == zz * 4 + b, sign, 0.0).astype(jnp.bfloat16)
                for half in value:
                    total += lax.dot_general(pick, half, nt, preferred_element_type=jnp.float32)
            line_of[...] = total
            return carry

        lax.fori_loop(0, 2, planes, 0)

    def edges():
        line = split(line_of[...])
        line_re = product(line, both(cos_x))
        line_im = -product(line, both(sin_x))
        for m in range(GX):
            at, off = HALF * (m // 16), 8 * (m % 16)
            re, im = line_re[:, at : at + HALF], line_im[:, at : at + HALF]
            tile = jnp.where(lane < 8, pltpu.roll(re, (HALF - off) % HALF, 1), 0.0)
            tile = jnp.where((lane >= 8) & (lane < 16), pltpu.roll(re, (HALF + 8 - off) % HALF, 1), tile)
            tile = jnp.where((lane >= 64) & (lane < 72), pltpu.roll(im, (HALF + 64 - off) % HALF, 1), tile)
            tile = jnp.where((lane >= 72) & (lane < 80), pltpu.roll(im, (HALF + 72 - off) % HALF, 1), tile)
            sent[m * SENT + 32 : m * SENT + 40, :] = tile

    def inverse(zz, last):
        def modes_of(b):
            parts = []
            for part in range(2):
                pieces = []
                for t in range(4):
                    for r in range(2):
                        for m in range(0, GX, ROWS):
                            row = m * BACK + (4 * t + 2 * zz + part) * ROWS + r * 4
                            pieces.append(back[pl.ds(row + b, ROWS, stride=BACK), :])
                parts.append(jnp.concatenate(pieces, axis=0))
            return split(jnp.concatenate(parts, axis=1))

        def planes(pair, carry):
            both_b = (2 * pair, 2 * pair + 1)
            modes = [modes_of(b) for b in both_b]
            us = [product(both(cos_cols), mode) for mode in modes]
            vs = [product(both(sin_cols), mode) for mode in modes]
            rows = [
                split(jnp.concatenate([u[:, :HALF] - v[:, HALF:], u[:, HALF:] + v[:, :HALF]], axis=1))
                for u, v in zip(us, vs)
            ]
            for b, row in zip(both_b, rows):
                value = product(row, both(back_y))
                field[zz, b] = value if last else value * coeff[zz]
            return carry

        lax.fori_loop(0, 2, planes, 0)

    def gather():
        def one(block, carry):
            for src, zz in [(4 * block + i, zz) for i in range(4) for zz in range(2)]:
                base = src * SENT
                line = tile_of(spec, base + 4 * ROWS)
                col = line if zz == 0 else pltpu.roll(line, 4, 0)
                col_re = jnp.where(lane < 16, col, 0.0)
                col_im = jnp.where(lane < 16, pltpu.roll(col, 64, 1), 0.0)
                espec[src, zz] = jnp.where(upper, col_re, pltpu.roll(tile_of(spec, base + spot(0, zz, 0) * ROWS), 4, 0))
                espec[src, 2 + zz] = jnp.where(
                    upper, col_im, pltpu.roll(tile_of(spec, base + spot(0, zz, 1) * ROWS), 4, 0)
                )
            return carry

        lax.fori_loop(0, GX // 4, one, 0)

    mean = jnp.where(upper & (gx == HALF // ROWS), 0.5, 0.0)

    def sweep(s, t, first, start_re, start_im):
        edge = t == 4
        inv = [(alpha[t, first + d, 0], alpha[t, first + d, 1]) for d in range(6)]

        def cells(step, psi):
            src = (GX - 1 - step) if first == 0 else step
            psi = list(psi)
            for zz in (1, 0) if first == 0 else (0, 1):
                z = 2 * src + zz
                if edge:
                    s_re, s_im = espec[src, zz], espec[src, 2 + zz]
                    g = [edge_goal[z, c] for c in range(2)]
                else:
                    s_re = tile_of(spec, src * SENT + spot(t, zz, 0) * ROWS)
                    s_im = tile_of(spec, src * SENT + spot(t, zz, 1) * ROWS)
                    g = [
                        jnp.where(upper, goal[z, c, 2 * t : 2 * t + 1], goal[z, c, 2 * t + 1 : 2 * t + 2])
                        for c in range(2)
                    ]
                s_re, s_im = s_re * rate, s_im * rate
                sums = [None, None]
                for d in range(6):
                    t_re = s_re + couple[d] * psi[2 * d]
                    t_im = s_im + couple[d] * psi[2 * d + 1]
                    p_re = inv[d][0] * t_re - inv[d][1] * t_im
                    p_im = inv[d][0] * t_im + inv[d][1] * t_re
                    psi[2 * d], psi[2 * d + 1] = p_re, p_im
                    sums = [p_re, p_im] if d == 0 else [sums[0] + p_re, sums[1] + p_im]
                    acc[z, first + d] += p_re * g[0] + p_im * g[1]
                if edge:
                    if first == 0:
                        enew[src, zz], enew[src, 2 + zz] = sums
                        continue
                    for c in range(2):
                        e = (enew[src, 2 * c + zz] + sums[c]) * (1.0 / 12.0)
                        enew[src, 2 * c + zz] = pltpu.roll(e, 4, 0)
                        h = 0.5 * (e + pltpu.roll(e, HALF - 8, 1))
                        epack[src, 2 * c + zz] = jnp.where(
                            upper, h, pltpu.roll(pltpu.roll(h, 4, 0), HALF - 1, 1)
                        )
                    continue
                for c in range(2):
                    rows = pl.ds(pl.multiple_of(src * BACK + (4 * t + 2 * zz + c) * ROWS, ROWS), ROWS)
                    if first == 0:
                        made[rows, :] = sums[c]
                        continue
                    total = (made[rows, :] + sums[c]) * (1.0 / 12.0)
                    if t == 0:
                        total = total + mean * (enew[src, 2 * c + zz] - total)
                    x = epack[src, 2 * (1 - c) + zz]
                    x = jnp.where(lane == 0, x if t == 0 else pltpu.roll(x, HALF - 2 * t, 1), 0.0)
                    made[rows, :] = total - x if c == 0 else total + x
            return tuple(psi)

        return lax.fori_loop(0, GX, cells, tuple([start_re, start_im] * 6))

    def down(s, t):
        psi = sweep(s, t, 0, zero, zero)
        at = 0 if t == 4 else 2 * t + 2
        for c in range(2):
            total = psi[c] * float(abs(COS[0]) / 12.0)
            for d in range(1, 6):
                total = total + psi[2 * d + c] * float(abs(COS[d]) / 12.0)
            flux[s, at + c] = total

    odd, second = sub % 2 == 1, sub % 4 >= 2

    def up(s, t):
        at = 0 if t == 4 else 2 * t + 2
        starts = []
        for c in range(2):
            total = flux[s, at + c] + others[s, 0, at + c] + others[s, 1, at + c] + others[s, 2, at + c]
            total = total + jnp.where(odd, pltpu.roll(total, 1, 0), pltpu.roll(total, ROWS - 1, 0))
            total = total + jnp.where(second, pltpu.roll(total, 2, 0), pltpu.roll(total, ROWS - 2, 0))
            starts.append(total * share)
        sweep(s, t, 6, *starts)

    def start_wall(s, message):
        for k in range(1, BA):
            wall_copy(s, message, k).start()

    def wait_wall(s, message):
        for k in range(1, BA):
            wall_copy(s, message, k).wait_recv()

    propagators()
    loads[2].wait()
    for s in range(2):
        lead_rows(s)
    pl.semaphore_wait(barrier, GX - 1 + BA - 1)
    for s in range(2):
        start_turn(s)

    def one_step(s, carry):
        line_of[...] = jnp.zeros_like(line_of)

        @pl.when(s > 0)
        def _():
            wait_homeward()
            sends_done(s - 1)
            inverse(0, False)

        @pl.when(s == 0)
        def _():
            loads[0].wait()

        forward(0)
        start_outward(0)

        @pl.when(s > 0)
        def _():
            inverse(1, False)

        @pl.when(s == 0)
        def _():
            for copy in (loads[1], loads[3]):
                copy.wait()

        forward(1)
        edges()

        @pl.when(s == 0)
        def _():
            start_share(0)
            start_share(1)

        start_outward(1)
        start_outward(2)
        fold(s)
        wait_outward(0)
        wait_outward(1)
        gather()
        down(s, 4)
        down(s, 0)
        start_wall(s, 0)
        start_outward(3)
        wait_outward(2)
        down(s, 1)
        start_wall(s, 1)
        start_outward(4)
        wait_wall(s, 0)
        up(s, 4)
        up(s, 0)
        start_homeward(0)
        for t in (1, 2):
            wait_outward(t + 2)
            down(s, t + 1)
            start_wall(s, t + 1)
            wait_wall(s, t)
            up(s, t)
            start_homeward(t)
        wait_wall(s, 3)
        up(s, 3)
        start_homeward(3)
        return carry

    lax.fori_loop(0, 2, one_step, 0)

    def reduce(src, carry):
        tile = zero
        for zz in range(2):
            for d in range(12):
                total = jnp.sum(acc[2 * src + zz, d], axis=1, keepdims=True)
                tile = jnp.where(lane == zz * 12 + d, total, tile)
        gsum[src] = tile * (1.0 / N)
        return carry

    lax.fori_loop(0, GX, reduce, 0)
    over_peers(lambda k: grad_copy(k).start())
    wait_homeward()
    for zz in range(2):
        inverse(zz, True)
    over_peers(lambda k: grad_copy(k).wait())
    gall[gx] = gsum[gx]
    total = gall[0]
    for src in range(1, GX):
        total = total + gall[src]
    grads[...] = total
    sends_done(1)
    turns_done()


def program(phi, coeff, target, rates, speeds, shares):
    f32 = jnp.float32
    dma = pltpu.SemaphoreType.DMA
    tile = (ROWS, HALF)
    hbm, local = pl.BlockSpec(memory_space=pl.ANY), pl.BlockSpec(memory_space=pltpu.VMEM)
    return pl.pallas_call(
        kernel,
        out_shape=[jax.ShapeDtypeStruct((2, 4, N, N), f32), jax.ShapeDtypeStruct(tile, f32)],
        in_specs=[hbm] * 3 + [pl.BlockSpec(memory_space=pltpu.SMEM)] * 3 + [local] * TABLES,
        out_specs=[local, local],
        scratch_shapes=[
            pltpu.VMEM((2, N, N), f32),
            pltpu.VMEM((2, 2, 64, ROWS, N), f32),
            pltpu.VMEM((2, 2, 64) + tile, f32),
            pltpu.VMEM((2, 2, 64, HALF), f32),
            pltpu.VMEM((2, 2, 64, HALF), f32),
            pltpu.VMEM((64, 2) + tile, f32),
            pltpu.VMEM((64, 2) + tile, f32),
            pltpu.VMEM((5, 12, 2) + tile, f32),
            pltpu.VMEM((GX * SENT, HALF), f32),
            pltpu.VMEM((GX * SENT, HALF), f32),
            pltpu.VMEM((GX * BACK, HALF), f32),
            pltpu.VMEM((GX * BACK, HALF), f32),
            pltpu.VMEM((64, 12) + tile, f32),
            pltpu.VMEM((GX, 4) + tile, f32),
            pltpu.VMEM((GX, 4) + tile, f32),
            pltpu.VMEM((GX, 4) + tile, f32),
            pltpu.VMEM((2, 10) + tile, f32),
            pltpu.VMEM((2, 3, 10) + tile, f32),
            pltpu.VMEM((GX,) + tile, f32),
            pltpu.VMEM((GX,) + tile, f32),
            pltpu.VMEM((ROWS, N), f32),
            dma((4,)),
            dma((len(OUTWARD),)),
            dma((len(HOMEWARD),)),
            dma((len(OUTWARD), GX)),
            dma((len(OUTWARD), GX)),
            dma((len(HOMEWARD), GX)),
            dma((len(HOMEWARD), GX)),
            dma((2, len(FLUXES), BA - 1)),
            dma((2, len(FLUXES), BA - 1)),
            dma((GX,)),
            dma((GX,)),
            dma((2,)),
            dma((2,)),
            dma((2,)),
            dma((2,)),
            dma((2, BA - 1)),
            dma((2, BA - 1)),
        ],
        compiler_params=pltpu.CompilerParams(collective_id=0, has_side_effects=True, vmem_limit_bytes=56 << 20),
        name="transport",
    )(phi, coeff, target, rates, speeds, shares, *tables())


def body(phi_start, coeff, forward, rates, speeds, shares):
    phi, sums = program(phi_start, coeff, forward, rates, speeds, shares)
    phi = phi * coeff[:, None]
    parts = sums[:, :24].reshape(2, 4, 2, 12)
    return (phi, jnp.transpose(parts[0] + parts[1], (1, 2, 0)))


def solution(mesh):
    in_specs = (
        P("gx", "ba", None, None),
        P("gx", None, None),
        P(None, None, None, "gx", None),
        P("ba"),
        P("ba"),
        P("ba"),
    )
    out_specs = (P("gx", "ba", None, None), P("gx", None, "ba"))
    return jax.shard_map(body, mesh=mesh, in_specs=in_specs, out_specs=out_specs, check_vma=False)
```

```python
import functools
import math

import jax
import jax.numpy as jnp
import numpy as np
from jax import lax
from jax.experimental import pallas as pl
from jax.experimental.pallas import tpu as pltpu
from jax.sharding import PartitionSpec as P

MESH = pl.DeviceIdType.MESH
N = 256
HALF = 128
GX = 32
BA = 4
ROWS = 8
BASE = 1.5 * 2.0 * math.pi / N


def quadrature():
    level = np.arange(6)
    polar = 0.2 + 0.15 * level
    cosine = np.concatenate([-polar, polar])
    azimuth = np.concatenate([level * (math.pi / 3.0) + math.pi / 6.0, level * (math.pi / 3.0)])
    sine = np.sqrt(1.0 - cosine * cosine)
    return cosine, sine * np.cos(azimuth), sine * np.sin(azimuth)


COS, SX, SY = quadrature()


def halves(table):
    table = jnp.asarray(table, jnp.float32)
    high = table.astype(jnp.bfloat16)
    return high, (table - high.astype(jnp.float32)).astype(jnp.bfloat16)


def np_halves(table):
    table = np.asarray(table, np.float32)
    high = table.astype(jnp.bfloat16)
    low = (table - high.astype(np.float32)).astype(jnp.bfloat16)
    return [jnp.asarray(high), jnp.asarray(low)]


def tables():
    index = np.arange(N)
    angle = (index[:, None] * index[None, :] % N) * (2.0 * np.pi / N)
    cos, sin = np.cos(angle) / 16.0, np.sin(angle) / 16.0
    rows = np.concatenate([cos[:, :HALF], -sin[:, :HALF]], axis=1)
    rows[:, HALF] = cos[:, HALF]
    back = np.concatenate([2.0 * cos[:HALF], -2.0 * sin[:HALF]], axis=0)
    back[0] = cos[0]
    back[HALF] = cos[HALF]
    order = np.arange(N).reshape(GX, ROWS).T.reshape(-1)
    stacks = [rows, back, cos, sin, cos[order], sin[order], cos[:, order], sin[:, order]]
    return [part for stack in stacks for part in np_halves(stack)]


def split(value):
    high = value.astype(jnp.bfloat16)
    return high, (value - high.astype(jnp.float32)).astype(jnp.bfloat16)


def product(left, right):
    lh, ll = left
    rh, rl = right
    dot = functools.partial(jnp.dot, preferred_element_type=jnp.float32)
    return dot(lh, rh) + (dot(ll, rh) + dot(lh, rl))


def stacked(lefts, right):
    dot = functools.partial(jnp.dot, preferred_element_type=jnp.float32)
    count = len(lefts)
    first = dot(jnp.concatenate([left[0] for left in lefts] + [left[1] for left in lefts], axis=0), right[0])
    second = dot(jnp.concatenate([left[0] for left in lefts], axis=0), right[1])
    cut = [slice(N * i, N * (i + 1)) for i in range(2 * count)]
    return [first[cut[i]] + (first[cut[count + i]] + second[cut[i]]) for i in range(count)]


SENT = 136
BACK = 128
OUTWARD = ((0, 2), (2, 3), (5, 4), (9, 4), (13, 4))
HOMEWARD = ((0, 4), (4, 4), (8, 4), (12, 4))
FLUXES = ((0, 4), (4, 2), (6, 2), (8, 2))
TABLES = 16


def spot(t, zz, part):
    return 4 * t + 2 * zz + part + (1 if t > 0 else 0)


def tile_of(ref, row):
    return ref[pl.ds(pl.multiple_of(row, ROWS), ROWS), :]


def kernel(phi, coeff_in, target, rates, speeds, shares, *rest):
    names = [rest[2 * i : 2 * i + 2] for i in range(TABLES // 2)]
    wave_y, back_y, cos_x, sin_x, cos_rows, sin_rows, cos_cols, sin_cols = names
    (field, grads, coeff, held, mirror, lead, lead_in, goal, edge_goal, alpha, sent, spec, made, back, acc, espec,
     enew, epack, flux, others, gsum, gall, line_of, load, own, own_back, send, recv, send_back, recv_back, send_flux,
     recv_flux, send_grad, recv_grad, send_turn, recv_turn, send_lead, recv_lead, send_share, recv_share) = rest[TABLES:]
    gx, ba = lax.axis_index("gx"), lax.axis_index("ba")
    barrier = pltpu.get_barrier_semaphore()

    def greet(k, carry):
        pl.semaphore_signal(barrier, inc=1, device_id=(lax.rem(gx + k, GX), ba), device_id_type=MESH)
        return carry

    lax.fori_loop(1, GX, greet, 0)
    for k in range(1, BA):
        pl.semaphore_signal(barrier, inc=1, device_id=(gx, lax.rem(ba + k, BA)), device_id_type=MESH)

    loads = [
        pltpu.make_async_copy(phi.at[0], field.at[0], load.at[0]),
        pltpu.make_async_copy(phi.at[1], field.at[1], load.at[1]),
        pltpu.make_async_copy(target, held, load.at[2]),
        pltpu.make_async_copy(coeff_in, coeff, load.at[3]),
    ]
    for copy in loads:
        copy.start()

    sub = lax.broadcasted_iota(jnp.int32, (ROWS, HALF), 0)
    lane = lax.broadcasted_iota(jnp.int32, (ROWS, HALF), 1)
    upper = sub < 4

    def by_band(values):
        spread = jnp.where(sub % 4 == 0, values[0], values[1])
        return jnp.where(sub % 4 >= 2, jnp.where(sub % 4 == 2, values[2], values[3]), spread)

    rate, speed, share = by_band(rates), by_band(speeds), by_band(shares)
    couple = [speed * float(abs(COS[d])) for d in range(6)]
    zero = jnp.zeros((ROWS, HALF), jnp.float32)

    def clear(z, carry):
        for d in range(12):
            acc[z, d] = zero
        return carry

    lax.fori_loop(0, 64, clear, 0)

    def signed(index):
        return (lax.rem(index + HALF, N) - HALF).astype(jnp.float32) * BASE

    def propagators():
        for t in range(5):
            if t < 4:
                fx, fy = signed(gx * ROWS + 2 * t + sub // 4), signed(lane)
            else:
                kx = gx * ROWS + lane % ROWS
                line = signed(kx)
                line = jnp.where((lane >= 8) & (kx == HALF), -line, line)
                fx = jnp.where(upper, line, HALF * BASE)
                fy = jnp.where(upper, jnp.where(lane < 8, -HALF * BASE, HALF * BASE), signed(lane))
            for d in range(12):
                wave = speed * (fx * float(SX[d]) + fy * float(SY[d]))
                real = rate + speed * float(abs(COS[d]))
                denom = real * real + wave * wave
                alpha[t, d, 0] = real / denom
                alpha[t, d, 1] = -wave / denom

    partner, first_row = GX - 1 - gx, lax.rem(GX - gx, GX)
    quarter = pl.ds(pl.multiple_of(ba * 16, 16), 16)

    def turn_copy(s):
        return pltpu.make_async_remote_copy(
            src_ref=held.at[s, :, quarter, :, pl.ds(HALF, HALF)],
            dst_ref=mirror.at[s, :, quarter],
            send_sem=send_turn.at[s],
            recv_sem=recv_turn.at[s],
            device_id=(partner, ba),
            device_id_type=MESH,
        )

    def share_copy(s, k):
        return pltpu.make_async_remote_copy(
            src_ref=mirror.at[s, :, quarter],
            dst_ref=mirror.at[s, :, quarter],
            send_sem=send_share.at[s, k - 1],
            recv_sem=recv_share.at[s, k - 1],
            device_id=(gx, lax.rem(ba + k, BA)),
            device_id_type=MESH,
        )

    def lead_copy(s):
        return pltpu.make_async_remote_copy(
            src_ref=lead.at[s],
            dst_ref=lead_in.at[s],
            send_sem=send_lead.at[s],
            recv_sem=recv_lead.at[s],
            device_id=(first_row, ba),
            device_id_type=MESH,
        )

    def lead_rows(s):
        for c in range(2):
            lead[s, c] = held[s, c, :, 0, HALF:]

    def start_turn(s):
        turn_copy(s).start()

        @pl.when(first_row != gx)
        def _():
            lead_copy(s).start()

    def start_share(s):
        turn_copy(s).wait_recv()
        for k in range(1, BA):
            share_copy(s, k).start()

    def fold(s):
        for k in range(1, BA):
            share_copy(s, k).wait_recv()

        @pl.when(first_row != gx)
        def _():
            lead_copy(s).wait_recv()

        @pl.when(first_row == gx)
        def _():
            lead_in[s] = lead[s]

        lanes = lax.rem(HALF - lane, HALF)
        rows = lax.rem(ROWS - sub, ROWS)
        keep = (lane > 0) & ((gx != HALF // ROWS) | (sub > 0))
        alone = (lane > 0) & (gx == HALF // ROWS)

        def cell(block, carry):
            for z, c in [(8 * block + i, c) for i in range(8) for c in range(2)]:
                tile = jnp.where(sub == 0, lead_in[s, c, pl.ds(z, 1), :], mirror[s, c, z])
                tile = jnp.take_along_axis(jnp.take_along_axis(tile, lanes, axis=1), rows, axis=0)
                tile = jnp.where(keep, tile, 0.0)
                low, high = held[s, c, z, :, :HALF], held[s, c, z, :, HALF:]
                goal[z, c] = low + tile if c == 0 else low - tile
                line = jnp.sum(jnp.where(lane == sub, jnp.broadcast_to(high[:, 0:1], (ROWS, HALF)), 0.0), axis=0, keepdims=True)
                other = jnp.where(alone, jnp.take_along_axis(high, lanes, axis=1), 0.0)
                other = other[0:1] if c == 0 else -other[0:1]
                edge_goal[z, c] = jnp.where(upper, line, other)
            return carry

        lax.fori_loop(0, 8, cell, 0)

    def turns_done():
        for s in range(2):
            turn_copy(s).wait_send()
            for k in range(1, BA):
                share_copy(s, k).wait_send()

            @pl.when(first_row != gx)
            def _():
                lead_copy(s).wait_send()

    def outward(message, k):
        first, count = OUTWARD[message]
        to = lax.rem(gx + k, GX)
        return pltpu.make_async_remote_copy(
            src_ref=sent.at[pl.ds(pl.multiple_of(to * SENT + first * ROWS, ROWS), count * ROWS), :],
            dst_ref=spec.at[pl.ds(pl.multiple_of(gx * SENT + first * ROWS, ROWS), count * ROWS), :],
            send_sem=send.at[message, k],
            recv_sem=recv.at[message, k],
            device_id=(to, ba),
            device_id_type=MESH,
        )

    def outward_own(message):
        first, count = OUTWARD[message]
        rows = pl.ds(pl.multiple_of(gx * SENT + first * ROWS, ROWS), count * ROWS)
        return pltpu.make_async_copy(sent.at[rows, :], spec.at[rows, :], own.at[message])

    def homeward(message, k):
        first, count = HOMEWARD[message]
        to = lax.rem(gx + k, GX)
        return pltpu.make_async_remote_copy(
            src_ref=made.at[pl.ds(pl.multiple_of(to * BACK + first * ROWS, ROWS), count * ROWS), :],
            dst_ref=back.at[pl.ds(pl.multiple_of(gx * BACK + first * ROWS, ROWS), count * ROWS), :],
            send_sem=send_back.at[message, k],
            recv_sem=recv_back.at[message, k],
            device_id=(to, ba),
            device_id_type=MESH,
        )

    def homeward_own(message):
        first, count = HOMEWARD[message]
        rows = pl.ds(pl.multiple_of(gx * BACK + first * ROWS, ROWS), count * ROWS)
        return pltpu.make_async_copy(made.at[rows, :], back.at[rows, :], own_back.at[message])

    def wall_copy(s, message, k):
        first, count = FLUXES[message]
        return pltpu.make_async_remote_copy(
            src_ref=flux.at[s, pl.ds(first, count)],
            dst_ref=others.at[s, k - 1, pl.ds(first, count)],
            send_sem=send_flux.at[s, message, k - 1],
            recv_sem=recv_flux.at[s, message, k - 1],
            device_id=(gx, lax.rem(ba + k, BA)),
            device_id_type=MESH,
        )

    def grad_copy(k):
        to = lax.rem(gx + k, GX)
        return pltpu.make_async_remote_copy(
            src_ref=gsum.at[to],
            dst_ref=gall.at[gx],
            send_sem=send_grad.at[k],
            recv_sem=recv_grad.at[k],
            device_id=(to, ba),
            device_id_type=MESH,
        )

    def over_peers(act):
        def one(k, carry):
            act(k)
            return carry

        lax.fori_loop(1, GX, one, 0)

    def start_outward(message):
        outward_own(message).start()
        over_peers(lambda k: outward(message, k).start())

    def wait_outward(message):
        outward_own(message).wait()
        over_peers(lambda k: outward(message, k).wait_recv())

    def start_homeward(message):
        homeward_own(message).start()
        over_peers(lambda k: homeward(message, k).start())

    def wait_homeward():
        for message in range(len(HOMEWARD)):
            homeward_own(message).wait()
            over_peers(lambda k: homeward(message, k).wait_recv())

    def sends_done(s):
        for message in range(len(OUTWARD)):
            over_peers(lambda k: outward(message, k).wait_send())
        for message in range(len(HOMEWARD)):
            over_peers(lambda k: homeward(message, k).wait_send())
        for message in range(len(FLUXES)):
            for k in range(1, BA):
                wall_copy(s, message, k).wait_send()

    inner = lax.broadcasted_iota(jnp.int32, (N, HALF), 1) != 0
    row8 = lax.broadcasted_iota(jnp.int32, (ROWS, N), 0)
    sign = jnp.where(lax.broadcasted_iota(jnp.int32, (ROWS, N), 1) % 2 == 0, 1.0 / 16.0, -1.0 / 16.0)

    def both(pair):
        return pair[0][...], pair[1][...]

    def forward(zz):
        def planes(pair, carry):
            both_b = (2 * pair, 2 * pair + 1)
            values = [split(field[zz, b]) for b in both_b]
            rows = [split(value) for value in stacked(values, both(wave_y))]
            uvs = [stacked((both(cos_rows), both(sin_rows)), row) for row in rows]
            for b, (u, v) in zip(both_b, uvs):
                re = u[:, :HALF] + jnp.where(inner, v[:, HALF:], 0.0)
                im = jnp.where(inner, u[:, HALF:], 0.0) - v[:, :HALF]
                for t in range(4):
                    for r in range(2):
                        for m in range(0, GX, ROWS):
                            at = (2 * t + r) * GX + m
                            for part, value in ((0, re), (1, im)):
                                row = m * SENT + spot(t, zz, part) * ROWS + r * 4
                                sent[pl.ds(row + b, ROWS, stride=SENT), :] = value[at : at + ROWS]
            nt = (((1,), (1,)), ((), ()))
            total = line_of[...]
            for b, value in zip(both_b, values):
                pick = jnp.where(row8 == zz * 4 + b, sign, 0.0).astype(jnp.bfloat16)
                for half in value:
                    total += lax.dot_general(pick, half, nt, preferred_element_type=jnp.float32)
            line_of[...] = total
            return carry

        lax.fori_loop(0, 2, planes, 0)

    def edges():
        line = split(line_of[...])
        line_re = product(line, both(cos_x))
        line_im = -product(line, both(sin_x))
        for m in range(GX):
            at, off = HALF * (m // 16), 8 * (m % 16)
            re, im = line_re[:, at : at + HALF], line_im[:, at : at + HALF]
            tile = jnp.where(lane < 8, pltpu.roll(re, (HALF - off) % HALF, 1), 0.0)
            tile = jnp.where((lane >= 8) & (lane < 16), pltpu.roll(re, (HALF + 8 - off) % HALF, 1), tile)
            tile = jnp.where((lane >= 64) & (lane < 72), pltpu.roll(im, (HALF + 64 - off) % HALF, 1), tile)
            tile = jnp.where((lane >= 72) & (lane < 80), pltpu.roll(im, (HALF + 72 - off) % HALF, 1), tile)
            sent[m * SENT + 32 : m * SENT + 40, :] = tile

    def inverse(zz, last):
        def modes_of(b):
            parts = []
            for part in range(2):
                pieces = []
                for t in range(4):
                    for r in range(2):
                        for m in range(0, GX, ROWS):
                            row = m * BACK + (4 * t + 2 * zz + part) * ROWS + r * 4
                            pieces.append(back[pl.ds(row + b, ROWS, stride=BACK), :])
                parts.append(jnp.concatenate(pieces, axis=0))
            return split(jnp.concatenate(parts, axis=1))

        def planes(pair, carry):
            both_b = (2 * pair, 2 * pair + 1)
            modes = [modes_of(b) for b in both_b]
            uvs = [stacked((both(cos_cols), both(sin_cols)), mode) for mode in modes]
            rows = [
                split(jnp.concatenate([u[:, :HALF] - v[:, HALF:], u[:, HALF:] + v[:, :HALF]], axis=1))
                for u, v in uvs
            ]
            for b, value in zip(both_b, [product(row, both(back_y)) for row in rows]):
                field[zz, b] = value if last else value * coeff[zz]
            return carry

        lax.fori_loop(0, 2, planes, 0)

    def gather():
        def one(block, carry):
            for src, zz in [(4 * block + i, zz) for i in range(4) for zz in range(2)]:
                base = src * SENT
                line = tile_of(spec, base + 4 * ROWS)
                col = line if zz == 0 else pltpu.roll(line, 4, 0)
                col_re = jnp.where(lane < 16, col, 0.0)
                col_im = jnp.where(lane < 16, pltpu.roll(col, 64, 1), 0.0)
                espec[src, zz] = jnp.where(upper, col_re, pltpu.roll(tile_of(spec, base + spot(0, zz, 0) * ROWS), 4, 0))
                espec[src, 2 + zz] = jnp.where(
                    upper, col_im, pltpu.roll(tile_of(spec, base + spot(0, zz, 1) * ROWS), 4, 0)
                )
            return carry

        lax.fori_loop(0, GX // 4, one, 0)

    mean = jnp.where(upper & (gx == HALF // ROWS), 0.5, 0.0)

    def sweep(s, t, first, start_re, start_im):
        edge = t == 4
        inv = [(alpha[t, first + d, 0], alpha[t, first + d, 1]) for d in range(6)]

        def cells(step, psi):
            src = (GX - 1 - step) if first == 0 else step
            psi = list(psi)
            for zz in (1, 0) if first == 0 else (0, 1):
                z = 2 * src + zz
                if edge:
                    s_re, s_im = espec[src, zz], espec[src, 2 + zz]
                    g = [edge_goal[z, c] for c in range(2)]
                else:
                    s_re = tile_of(spec, src * SENT + spot(t, zz, 0) * ROWS)
                    s_im = tile_of(spec, src * SENT + spot(t, zz, 1) * ROWS)
                    g = [
                        jnp.where(upper, goal[z, c, 2 * t : 2 * t + 1], goal[z, c, 2 * t + 1 : 2 * t + 2])
                        for c in range(2)
                    ]
                s_re, s_im = s_re * rate, s_im * rate
                sums = [None, None]
                for d in range(6):
                    t_re = s_re + couple[d] * psi[2 * d]
                    t_im = s_im + couple[d] * psi[2 * d + 1]
                    p_re = inv[d][0] * t_re - inv[d][1] * t_im
                    p_im = inv[d][0] * t_im + inv[d][1] * t_re
                    psi[2 * d], psi[2 * d + 1] = p_re, p_im
                    sums = [p_re, p_im] if d == 0 else [sums[0] + p_re, sums[1] + p_im]
                    acc[z, first + d] += p_re * g[0] + p_im * g[1]
                if edge:
                    if first == 0:
                        enew[src, zz], enew[src, 2 + zz] = sums
                        continue
                    for c in range(2):
                        e = (enew[src, 2 * c + zz] + sums[c]) * (1.0 / 12.0)
                        enew[src, 2 * c + zz] = pltpu.roll(e, 4, 0)
                        h = 0.5 * (e + pltpu.roll(e, HALF - 8, 1))
                        epack[src, 2 * c + zz] = jnp.where(
                            upper, h, pltpu.roll(pltpu.roll(h, 4, 0), HALF - 1, 1)
                        )
                    continue
                for c in range(2):
                    rows = pl.ds(pl.multiple_of(src * BACK + (4 * t + 2 * zz + c) * ROWS, ROWS), ROWS)
                    if first == 0:
                        made[rows, :] = sums[c]
                        continue
                    total = (made[rows, :] + sums[c]) * (1.0 / 12.0)
                    if t == 0:
                        total = total + mean * (enew[src, 2 * c + zz] - total)
                    x = epack[src, 2 * (1 - c) + zz]
                    x = jnp.where(lane == 0, x if t == 0 else pltpu.roll(x, HALF - 2 * t, 1), 0.0)
                    made[rows, :] = total - x if c == 0 else total + x
            return tuple(psi)

        return lax.fori_loop(0, GX, cells, tuple([start_re, start_im] * 6))

    def down(s, t):
        psi = sweep(s, t, 0, zero, zero)
        at = 0 if t == 4 else 2 * t + 2
        for c in range(2):
            total = psi[c] * float(abs(COS[0]) / 12.0)
            for d in range(1, 6):
                total = total + psi[2 * d + c] * float(abs(COS[d]) / 12.0)
            flux[s, at + c] = total

    odd, second = sub % 2 == 1, sub % 4 >= 2

    def up(s, t):
        at = 0 if t == 4 else 2 * t + 2
        starts = []
        for c in range(2):
            total = flux[s, at + c] + others[s, 0, at + c] + others[s, 1, at + c] + others[s, 2, at + c]
            total = total + jnp.where(odd, pltpu.roll(total, 1, 0), pltpu.roll(total, ROWS - 1, 0))
            total = total + jnp.where(second, pltpu.roll(total, 2, 0), pltpu.roll(total, ROWS - 2, 0))
            starts.append(total * share)
        sweep(s, t, 6, *starts)

    def start_wall(s, message):
        for k in range(1, BA):
            wall_copy(s, message, k).start()

    def wait_wall(s, message):
        for k in range(1, BA):
            wall_copy(s, message, k).wait_recv()

    propagators()
    loads[2].wait()
    for s in range(2):
        lead_rows(s)
    pl.semaphore_wait(barrier, GX - 1 + BA - 1)
    for s in range(2):
        start_turn(s)

    def one_step(s, carry):
        line_of[...] = jnp.zeros_like(line_of)

        @pl.when(s > 0)
        def _():
            wait_homeward()
            sends_done(s - 1)
            inverse(0, False)

        @pl.when(s == 0)
        def _():
            loads[0].wait()

        forward(0)
        start_outward(0)

        @pl.when(s > 0)
        def _():
            inverse(1, False)

        @pl.when(s == 0)
        def _():
            for copy in (loads[1], loads[3]):
                copy.wait()

        forward(1)
        edges()

        @pl.when(s == 0)
        def _():
            start_share(0)
            start_share(1)

        start_outward(1)
        start_outward(2)
        fold(s)
        wait_outward(0)
        wait_outward(1)
        gather()
        down(s, 4)
        down(s, 0)
        start_wall(s, 0)
        start_outward(3)
        wait_outward(2)
        down(s, 1)
        start_wall(s, 1)
        start_outward(4)
        wait_wall(s, 0)
        up(s, 4)
        up(s, 0)
        start_homeward(0)
        for t in (1, 2):
            wait_outward(t + 2)
            down(s, t + 1)
            start_wall(s, t + 1)
            wait_wall(s, t)
            up(s, t)
            start_homeward(t)
        wait_wall(s, 3)
        up(s, 3)
        start_homeward(3)
        return carry

    lax.fori_loop(0, 2, one_step, 0)

    def reduce(src, carry):
        tile = zero
        for zz in range(2):
            for d in range(12):
                total = jnp.sum(acc[2 * src + zz, d], axis=1, keepdims=True)
                tile = jnp.where(lane == zz * 12 + d, total, tile)
        gsum[src] = tile * (1.0 / N)
        return carry

    lax.fori_loop(0, GX, reduce, 0)
    over_peers(lambda k: grad_copy(k).start())
    wait_homeward()
    for zz in range(2):
        inverse(zz, True)
    over_peers(lambda k: grad_copy(k).wait())
    gall[gx] = gsum[gx]
    total = gall[0]
    for src in range(1, GX):
        total = total + gall[src]
    grads[...] = total
    sends_done(1)
    turns_done()


def program(phi, coeff, target, rates, speeds, shares):
    f32 = jnp.float32
    dma = pltpu.SemaphoreType.DMA
    tile = (ROWS, HALF)
    hbm, local = pl.BlockSpec(memory_space=pl.ANY), pl.BlockSpec(memory_space=pltpu.VMEM)
    return pl.pallas_call(
        kernel,
        out_shape=[jax.ShapeDtypeStruct((2, 4, N, N), f32), jax.ShapeDtypeStruct(tile, f32)],
        in_specs=[hbm] * 3 + [pl.BlockSpec(memory_space=pltpu.SMEM)] * 3 + [local] * TABLES,
        out_specs=[local, local],
        scratch_shapes=[
            pltpu.VMEM((2, N, N), f32),
            pltpu.VMEM((2, 2, 64, ROWS, N), f32),
            pltpu.VMEM((2, 2, 64) + tile, f32),
            pltpu.VMEM((2, 2, 64, HALF), f32),
            pltpu.VMEM((2, 2, 64, HALF), f32),
            pltpu.VMEM((64, 2) + tile, f32),
            pltpu.VMEM((64, 2) + tile, f32),
            pltpu.VMEM((5, 12, 2) + tile, f32),
            pltpu.VMEM((GX * SENT, HALF), f32),
            pltpu.VMEM((GX * SENT, HALF), f32),
            pltpu.VMEM((GX * BACK, HALF), f32),
            pltpu.VMEM((GX * BACK, HALF), f32),
            pltpu.VMEM((64, 12) + tile, f32),
            pltpu.VMEM((GX, 4) + tile, f32),
            pltpu.VMEM((GX, 4) + tile, f32),
            pltpu.VMEM((GX, 4) + tile, f32),
            pltpu.VMEM((2, 10) + tile, f32),
            pltpu.VMEM((2, 3, 10) + tile, f32),
            pltpu.VMEM((GX,) + tile, f32),
            pltpu.VMEM((GX,) + tile, f32),
            pltpu.VMEM((ROWS, N), f32),
            dma((4,)),
            dma((len(OUTWARD),)),
            dma((len(HOMEWARD),)),
            dma((len(OUTWARD), GX)),
            dma((len(OUTWARD), GX)),
            dma((len(HOMEWARD), GX)),
            dma((len(HOMEWARD), GX)),
            dma((2, len(FLUXES), BA - 1)),
            dma((2, len(FLUXES), BA - 1)),
            dma((GX,)),
            dma((GX,)),
            dma((2,)),
            dma((2,)),
            dma((2,)),
            dma((2,)),
            dma((2, BA - 1)),
            dma((2, BA - 1)),
        ],
        compiler_params=pltpu.CompilerParams(collective_id=0, has_side_effects=True, vmem_limit_bytes=56 << 20),
        name="transport",
    )(phi, coeff, target, rates, speeds, shares, *tables())


def body(phi_start, coeff, forward, rates, speeds, shares):
    phi, sums = program(phi_start, coeff, forward, rates, speeds, shares)
    phi = phi * coeff[:, None]
    parts = sums[:, :24].reshape(2, 4, 2, 12)
    return (phi, jnp.transpose(parts[0] + parts[1], (1, 2, 0)))


def solution(mesh):
    in_specs = (
        P("gx", "ba", None, None),
        P("gx", None, None),
        P(None, None, None, "gx", None),
        P("ba"),
        P("ba"),
        P("ba"),
    )
    out_specs = (P("gx", "ba", None, None), P("gx", None, "ba"))
    return jax.shard_map(body, mesh=mesh, in_specs=in_specs, out_specs=out_specs, check_vma=False)
```
